512 devices in a mesh: rows: 128 (over z, y, core), cent: 4 (over x).
Axes of the slice: x: 4, y: 8, z: 8, core: 2. Of those that a mesh axis runs over, the one named last changes fastest.
Arguments:
- embeddings: bfloat16 [131072, 768], P('rows'), may hold values from -6 to 6
- centroids: bfloat16 [4096, 768], P('cent'), may hold values from -0.21875 to 0.21875
- positions: int32 [131072], P('rows'), may hold values from 0 to 131071, as said below
- cluster_sizes: int32 [4096], replicated, may hold values from 1 to 1024, 131072 in all
Outputs:
- margin: float32 [131072], P('rows')
- prior_sim: float32 [131072], P(('rows', 'cent'))
The draws below stay inside these ranges and needn't reach their ends.
Inputs may be any that keep to these rules, and one draw needn't show every extreme that they name: positions is a permutation of the places. Call owner o the places o * 1024 to (o + 1) * 1024 - 1, and quarter c of index r of rows the rows r * 1024 + c * 256 to r * 1024 + (c + 1) * 256 - 1. The number of rows of quarter c of index r with places at owner o is 2 plus a term that depends only on c and on (o - r) modulo 128 and sums to zero over o; it is at most 4, and exactly that for some pair in every draw. `cluster_sizes`: the sizes sum to 131072; the largest is exactly 1024.
All inputs are finite; a program needn't handle non-finite values.
Results may differ from the reference program's by a relative error of at most 0.0012.
Values may be sent and summed in bfloat16 or wider, within the bound.
No kernel may reach another device: no remote copies, remote signals or barrier semaphores. Data moves between devices by JAX's collectives and lax.ppermute only.
A program may use at most 64 MiB of HBM per device.

```python
import math
import jax
import jax.numpy as jnp
import numpy as np
from jax import lax

D = 768
ROWS_DEV = 256
OWN = 1024
N_TOTAL = 131072
K_ALL = 4096
N_ROWS = 128
N_CENT = 4


def draw_positions(key, part):
    base_count = ROWS_DEV // N_ROWS
    block_rows = ROWS_DEV * N_CENT
    source_count = N_ROWS * N_CENT
    spare_count = N_ROWS - 1
    key_peak = jax.random.fold_in(key, 11)
    key_fall = jax.random.fold_in(key, 13)
    key_slot = jax.random.fold_in(key, 17)
    key_row = jax.random.fold_in(key, 19)
    peak_lag = jax.random.randint(key_peak, (N_CENT,), 0, N_ROWS)
    fall_order = jax.vmap(lambda subkey: jax.random.permutation(subkey, spare_count))(jax.random.split(key_fall, N_CENT))
    fall_count = base_count // spare_count + (fall_order < base_count % spare_count).astype(jnp.int32)
    delta_table = jnp.concatenate([jnp.full((N_CENT, 1), base_count, jnp.int32), -fall_count.astype(jnp.int32)], axis=1)
    row_grid = jnp.arange(N_ROWS)[:, None, None]
    cent_grid = jnp.arange(N_CENT)[None, :, None]
    owner_grid = jnp.arange(N_ROWS)[None, None, :]
    relative = (owner_grid - row_grid - peak_lag[cent_grid]) % N_ROWS
    cent_full = jnp.broadcast_to(cent_grid, relative.shape)
    counts = (base_count + delta_table[cent_full, relative]).astype(jnp.int32).reshape(source_count, N_ROWS)
    owners = jax.vmap(lambda count_row: jnp.repeat(jnp.arange(N_ROWS, dtype=jnp.int32), count_row, total_repeat_length=ROWS_DEV))(counts)
    within_start = jnp.cumsum(counts, axis=1) - counts
    inside = jnp.arange(ROWS_DEV, dtype=jnp.int32)[None, :] - jnp.take_along_axis(within_start, owners, axis=1)
    source_start = jnp.cumsum(counts, axis=0) - counts
    slot_index = jnp.take_along_axis(source_start, owners, axis=1) + inside
    shuffle = jax.vmap(lambda subkey: jax.random.permutation(subkey, block_rows))(jax.random.split(key_slot, N_ROWS))
    places = owners * block_rows + shuffle[owners, slot_index]
    mixing = jax.vmap(lambda subkey: jax.random.permutation(subkey, ROWS_DEV))(jax.random.split(key_row, source_count))
    places = jnp.take_along_axis(places, mixing, axis=1)
    return places.reshape(-1).astype(jnp.int32)


def block_scale(stream_key, extent, shards, least, largest):
    factor_of = 1.0
    for position, shards_of in shards:
        heights = jax.random.uniform(jax.random.fold_in(jax.random.fold_in(stream_key, 6), position), (shards_of,), jnp.float32, least / len(shards), largest / len(shards))
        factor_of = factor_of * jnp.repeat(jnp.exp(heights), extent[position] // shards_of).reshape((-1,) + (1,) * (len(extent) - 1 - position))
    return factor_of


def profile(count, total, limit, skew):
    weights = [(1 << 20) // math.isqrt(rank ** skew) + 1 for rank in range(2, count + 1)]
    rest, given = total - limit - (count - 1), [1] * (count - 1)
    while rest > 0:
        movable = [i for i in range(count - 1) if given[i] < limit]
        pool, left = sum([weights[i] for i in movable]), rest
        for i in movable:
            more = min(limit - given[i], max(1, left * weights[i] // pool), rest)
            given[i] = given[i] + more
            rest = rest - more
    return np.array([limit] + given)


def ragged(stream_key, amount, total, reach, skew):
    if amount == 2:
        one = jax.random.randint(stream_key, (), max(1, total - reach), min(reach, total - 1) + 1)
        return jnp.stack([one, total - one])
    tallies = jnp.asarray(profile(amount, total, reach, skew), jnp.int32)
    twos = (amount - 1) // 2
    donor, receiver = tallies[1:1 + 2 * twos:2], tallies[2:2 + 2 * twos:2]
    slack = jnp.minimum(donor - 1, reach - receiver)
    shifted = jax.random.randint(jax.random.fold_in(stream_key, 1), (twos,), 0, 1 << 20) % (slack + 1)
    tallies = tallies.at[1:1 + 2 * twos:2].set(donor - shifted).at[2:2 + 2 * twos:2].set(receiver + shifted)
    return tallies[jax.random.permutation(jax.random.fold_in(stream_key, 2), amount)]


def bell_draw(rng, extent, scale, reach, cuts=(), held_as=jnp.bfloat16):
    drawn = scale * jax.random.normal(rng, extent, jnp.float32)
    if cuts:
        drawn = drawn * block_scale(rng, extent, cuts, -0.22, 0.18)
    return jnp.clip(drawn, -reach, reach).astype(held_as)


def setup_inputs(seed: int = 0) -> dict:
    streams_of = jax.random.split(jax.random.key(seed), 5)
    return {
        "embeddings": bell_draw(streams_of[0], (N_TOTAL, D), 1.0, 6.0, ((0, 128),)),
        "centroids": bell_draw(streams_of[1], (K_ALL, D), D ** -0.5, 0.21875, ((0, 4),)),
        "positions": draw_positions(jax.random.fold_in(streams_of[4], 71), 0),
        "cluster_sizes": ragged(streams_of[3], K_ALL, N_TOTAL, OWN, 2).astype(jnp.int32),
    }


def reference(embeddings, centroids, positions, cluster_sizes):
    total_rows = embeddings.shape[0]
    block_rows = ROWS_DEV * N_CENT
    block_count = total_rows // block_rows
    floats = embeddings.astype(jnp.float32)
    normed = (floats * lax.rsqrt(lax.optimization_barrier(jnp.sum(floats * floats, axis=-1, keepdims=True)) + 1e-06)).astype(jnp.bfloat16)
    cluster_ends = jnp.cumsum(cluster_sizes).astype(jnp.int32)
    assigned = jnp.searchsorted(cluster_ends, positions, side='right').astype(jnp.int32)
    row_blocks = normed.reshape(block_count, block_rows, D)
    assigned_blocks = assigned.reshape(block_count, block_rows)

    def score_block(pair):
        block_data, block_assigned = pair
        scores = jnp.dot(block_data, centroids.T, preferred_element_type=jnp.float32)
        best_sim = lax.optimization_barrier(jnp.max(scores, axis=1))
        picked = jnp.take_along_axis(scores, block_assigned[:, None], axis=1)[:, 0]
        return best_sim - picked
    margin = lax.map(score_block, (row_blocks, assigned_blocks)).reshape(total_rows)
    ordered = jnp.zeros_like(normed).at[positions].set(normed)
    padded = jnp.concatenate([jnp.zeros((block_rows, D), normed.dtype), ordered], axis=0)

    def prior_block(block_index):
        first_place = (block_index * block_rows).astype(jnp.int32)
        queries = lax.dynamic_slice_in_dim(ordered, first_place, block_rows, 0)
        keys_all = lax.dynamic_slice_in_dim(padded, first_place, 2 * block_rows, 0)
        key_places = (first_place - block_rows + jnp.arange(2 * block_rows)).astype(jnp.int32)
        query_places = (first_place + jnp.arange(block_rows)).astype(jnp.int32)
        key_cluster = jnp.searchsorted(cluster_ends, key_places, side='right').astype(jnp.int32)
        query_cluster = jnp.searchsorted(cluster_ends, query_places, side='right').astype(jnp.int32)
        similarity = jnp.dot(queries, keys_all.T, preferred_element_type=jnp.float32)
        allowed = (key_cluster[None, :] == query_cluster[:, None]) & (key_places[None, :] < query_places[:, None]) & (key_places[None, :] >= 0)
        return lax.optimization_barrier(jnp.max(jnp.where(allowed, similarity, -1.0), axis=1))
    prior_sim = lax.map(prior_block, jnp.arange(block_count, dtype=jnp.int32)).reshape(total_rows)
    return (margin, prior_sim)
```

```python
import jax
import jax.numpy as jnp
from jax import lax
from jax.experimental import pallas as pl
from jax.experimental.pallas import tpu as pltpu
from jax.sharding import PartitionSpec as P

SLOTS = 4
LANES = 128
TAG_BASE = 32
TAG_ROWS = 8


def rotated(shard, axis, by):
    peers = lax.axis_size(axis)
    return lax.ppermute(shard, axis, [(i, (i + by) % peers) for i in range(peers)])


def iota(shape, dim):
    return lax.broadcasted_iota(jnp.int32, shape, dim)


def as_column(row):
    size = row.shape[1]
    eye = iota((size, size), 0) == iota((size, size), 1)
    return jnp.sum(jnp.where(eye, row, jnp.zeros_like(row)), axis=1, keepdims=True)


def as_row(column):
    size = column.shape[0]
    eye = iota((size, size), 0) == iota((size, size), 1)
    return jnp.sum(jnp.where(eye, column, jnp.zeros_like(column)), axis=0, keepdims=True)


def dot(left, right, left_dim, right_dim):
    return lax.dot_general(
        left, right, (((left_dim,), (right_dim,)), ((), ())), preferred_element_type=jnp.float32
    )


def normalise(rows):
    floats = rows.astype(jnp.float32)
    return (floats * lax.rsqrt(jnp.sum(floats * floats, axis=-1, keepdims=True) + 1e-06)).astype(
        jnp.bfloat16
    )


def pack_kernel(cent_ref, rows_ref, places_ref, out_ref, *, owner_rows):
    normed = normalise(rows_ref[...])
    count, features = normed.shape
    slots = out_ref.shape[0]
    places = places_ref[0]
    owners = places // owner_rows
    owner_column = as_column(owners)
    earlier = (owner_column == owners) & (iota((count, count), 0) < iota((count, count), 1))
    rank = jnp.sum(earlier.astype(jnp.int32), axis=0, keepdims=True)
    slot = owners * SLOTS + rank
    chosen = (iota((slots, count), 0) == slot).astype(jnp.bfloat16)
    local = as_column(places % owner_rows)
    lane = iota((count, LANES), 1)
    tags = jnp.where(lane == 0, local // TAG_BASE + 1, jnp.where(lane == 1, local % TAG_BASE, 0))
    tags = tags.astype(jnp.float32).astype(jnp.bfloat16)
    out_ref[:, :features] = dot(chosen, normed, 1, 0).astype(jnp.bfloat16)
    out_ref[:, features:] = dot(chosen, tags, 1, 0).astype(jnp.bfloat16)


def pack(rows, places, cent_index, owners, owner_rows, quarters):
    count, features = rows.shape
    quarter = count // quarters
    slots = owners * SLOTS
    return pl.pallas_call(
        lambda *refs: pack_kernel(*refs, owner_rows=owner_rows),
        grid_spec=pltpu.PrefetchScalarGridSpec(
            num_scalar_prefetch=1,
            grid=(1,),
            in_specs=[
                pl.BlockSpec((quarter, features), lambda i, cent: (cent[0], 0)),
                pl.BlockSpec((1, 1, quarter), lambda i, cent: (cent[0], 0, 0)),
            ],
            out_specs=pl.BlockSpec((slots, features + LANES), lambda i, cent: (0, 0)),
        ),
        out_shape=jax.ShapeDtypeStruct((slots, features + LANES), jnp.bfloat16),
        name="pack",
    )(cent_index[None], rows, places.reshape(quarters, 1, quarter))


def compact_kernel(got_ref, out_ref):
    slots = got_ref.shape[0]
    features = out_ref.shape[1]
    count = out_ref.shape[0] - TAG_ROWS
    tags = got_ref[:, features:].astype(jnp.float32)
    high = tags[:, 0:1]
    low = tags[:, 1:2]
    filled = high > 0.5
    before = (iota((slots, slots), 1) < iota((slots, slots), 0)).astype(jnp.bfloat16)
    marks = jnp.broadcast_to(filled.astype(jnp.float32), (slots, LANES)).astype(jnp.bfloat16)
    rank = dot(before, marks, 1, 0)[:, 0:1].astype(jnp.int32)
    chosen = (rank == iota((slots, count), 1)) & filled
    out_ref[:count, :] = dot(
        chosen.astype(jnp.bfloat16), got_ref[:, :features], 0, 0
    ).astype(jnp.bfloat16)
    high_row = jnp.sum(jnp.where(chosen, high - 1.0, 0.0), axis=0, keepdims=True)
    low_row = jnp.sum(jnp.where(chosen, low, 0.0), axis=0, keepdims=True)
    spare = jnp.zeros((1, features - 2 * count), jnp.float32)
    row = jnp.concatenate([high_row, low_row, spare], axis=1)
    out_ref[count:, :] = jnp.broadcast_to(row, (TAG_ROWS, features)).astype(jnp.bfloat16)


def compact(got, count, features):
    return pl.pallas_call(
        compact_kernel,
        out_shape=jax.ShapeDtypeStruct((count + TAG_ROWS, features), jnp.bfloat16),
        name="compact",
    )(got)


def key_places(part_ref, count):
    tags = part_ref[count:, :].astype(jnp.float32)
    row = tags[0:1, :count] * float(TAG_BASE) + tags[0:1, count : 2 * count]
    return as_column(row.astype(jnp.int32))


def own_kernel(first_ref, starts_ref, *refs):
    *part_refs, queries_ref, best_ref = refs
    count = queries_ref.shape[0]
    query_places = first_ref[0] + iota((1, count), 1)
    starts = starts_ref[...]
    columns = [key_places(part, count) for part in part_refs]
    queries = jnp.zeros(queries_ref.shape, jnp.float32)
    for column, part in zip(columns, part_refs):
        chosen = (column == query_places).astype(jnp.bfloat16)
        queries = queries + dot(chosen, part[:count, :], 0, 0)
    queries = queries.astype(jnp.bfloat16)
    queries_ref[...] = queries
    best = jnp.full((1, count), -1.0, jnp.float32)
    for column, part in zip(columns, part_refs):
        similarity = dot(part[:count, :], queries, 1, 1)
        allowed = (column >= starts) & (column < query_places)
        masked = jnp.where(allowed, similarity, -1.0)
        best = jnp.maximum(best, jnp.max(masked, axis=0, keepdims=True))
    best_ref[...] = best


def previous_kernel(starts_ref, best_ref, queries_ref, *refs, owner_rows):
    *part_refs, out_ref = refs
    count = queries_ref.shape[0]
    starts = starts_ref[...]
    queries = queries_ref[...]
    best = best_ref[...]
    for part in part_refs:
        column = key_places(part, count) - owner_rows
        similarity = dot(part[:count, :], queries, 1, 1)
        masked = jnp.where(column >= starts, similarity, -1.0)
        best = jnp.maximum(best, jnp.max(masked, axis=0, keepdims=True))
    out_ref[...] = best


def on_device(embeddings, centroids, positions, cluster_sizes):
    block_rows, features = embeddings.shape
    row_count = lax.axis_size("rows")
    cent_count = lax.axis_size("cent")
    quarter = block_rows // cent_count
    slab_size = centroids.shape[0]
    row_index = lax.axis_index("rows")
    cent_index = lax.axis_index("cent")

    packed = pack(embeddings, positions, cent_index, row_count, block_rows, cent_count)
    got = lax.all_to_all(
        packed.reshape(row_count, SLOTS, -1), "rows", split_axis=0, concat_axis=0, tiled=True
    )

    cluster_ends = jnp.cumsum(cluster_sizes)
    cluster_starts = cluster_ends - cluster_sizes
    slab_ends = lax.dynamic_slice_in_dim(cluster_ends, cent_index * slab_size, slab_size)
    slab_starts = lax.dynamic_slice_in_dim(cluster_starts, cent_index * slab_size, slab_size)
    scores = lax.dot_general(
        normalise(embeddings),
        centroids,
        (((1,), (1,)), ((), ())),
        preferred_element_type=jnp.float32,
    )
    best_sim = jnp.max(scores, axis=1)
    assigned = (slab_starts[None, :] <= positions[:, None]) & (
        positions[:, None] < slab_ends[None, :]
    )
    picked = jnp.sum(jnp.where(assigned, scores, 0.0), axis=1)
    both = jnp.stack([best_sim, picked])
    for both_there in [rotated(both, "cent", by) for by in range(1, cent_count)]:
        best_sim = jnp.maximum(best_sim, both_there[0])
        picked = picked + both_there[1]
    margin = best_sim - picked

    base_place = row_index * block_rows
    first_local = cent_index * quarter
    query_places = base_place + first_local + jnp.arange(quarter, dtype=jnp.int32)
    started = jnp.where(cluster_starts[None, :] <= query_places[:, None], cluster_starts[None, :], 0)
    query_starts = (jnp.max(started, axis=1) - base_place)[None, :]

    mine = compact(got.reshape(row_count * SLOTS, -1), quarter, features)
    own_parts = [mine] + [rotated(mine, "cent", by) for by in (1, 3, 2)]
    previous_parts = [rotated(part, "rows", 1) for part in own_parts]
    queries, own_best = pl.pallas_call(
        own_kernel,
        in_specs=[pl.BlockSpec(memory_space=pltpu.SMEM)]
        + [pl.BlockSpec(memory_space=pltpu.VMEM)] * (1 + cent_count),
        out_shape=(
            jax.ShapeDtypeStruct((quarter, features), jnp.bfloat16),
            jax.ShapeDtypeStruct((1, quarter), jnp.float32),
        ),
        name="own",
    )(first_local[None], query_starts, *own_parts)
    prior_sim = pl.pallas_call(
        lambda *refs: previous_kernel(*refs, owner_rows=block_rows),
        out_shape=jax.ShapeDtypeStruct((1, quarter), jnp.float32),
        name="previous",
    )(query_starts, own_best, queries, *previous_parts)
    return (margin, prior_sim.reshape(quarter))


def solution(mesh):
    in_specs = (P("rows", None), P("cent", None), P("rows"), P())
    out_specs = (P("rows"), P(("rows", "cent")))
    return jax.shard_map(
        on_device, mesh=mesh, in_specs=in_specs, out_specs=out_specs, check_vma=False
    )
```

```python
import jax
import jax.numpy as jnp
from jax import lax
from jax.experimental import pallas as pl
from jax.experimental.pallas import tpu as pltpu
from jax.sharding import PartitionSpec as P

SLOTS = 4
LANES = 128
TAG_BASE = 32
PAIR_SLOTS = 6
PAIR_ROWS = 8
HELD = 264
PART = 272
NOWHERE = -4096


def rotated(shard, axis, by):
    peers = lax.axis_size(axis)
    return lax.ppermute(shard, axis, [(i, (i + by) % peers) for i in range(peers)])


def to_next_owner(shard):
    row_count = lax.axis_size("rows")
    return lax.ppermute(shard, "rows", [(row, row + 1) for row in range(row_count - 1)])


def from_holders(shard, cent_by, row_by):
    row_count, cent_count = lax.axis_size("rows"), lax.axis_size("cent")
    pairs = []
    for row in range(row_count):
        for cent in range(cent_count):
            target_row = (row ^ (cent // 2)) + row_by
            target_cent = (cent + cent_by) % cent_count
            if target_row < row_count:
                pairs.append((row * cent_count + cent, target_row * cent_count + target_cent))
    return lax.ppermute(shard, ("rows", "cent"), pairs)


def iota(shape, dim):
    return lax.broadcasted_iota(jnp.int32, shape, dim)


def as_column(row):
    size = row.shape[1]
    eye = iota((size, size), 0) == iota((size, size), 1)
    return jnp.sum(jnp.where(eye, row, jnp.zeros_like(row)), axis=1, keepdims=True)


def dot(left, right, left_dim, right_dim):
    return lax.dot_general(
        left, right, (((left_dim,), (right_dim,)), ((), ())), preferred_element_type=jnp.float32
    )


def normalise(rows):
    floats = rows.astype(jnp.float32)
    return (floats * lax.rsqrt(jnp.sum(floats * floats, axis=-1, keepdims=True) + 1e-06)).astype(
        jnp.bfloat16
    )


def tag_rows(local):
    return local // TAG_BASE + 1, local % TAG_BASE


def pack_pairs_kernel(row_ref, cent_ref, rows_ref, places_ref, out_ref, fits_ref, *, owner_rows):
    row_index = row_ref[0]
    sibling = cent_ref[0] // 2
    half = cent_ref[0] % 2
    count, features = rows_ref.shape
    slots = out_ref.shape[0]
    places = places_ref[...]
    owners = places // owner_rows
    owner_count = count // PAIR_ROWS
    step = 256
    earlier = (iota((step, step), 0) < iota((step, step), 1)).astype(jnp.bfloat16)
    so_far = jnp.zeros((owner_count, 1), jnp.float32)
    ranks = []
    for first in range(0, count, step):
        here = iota((owner_count, step), 0) == owners[:, first : first + step]
        marks = here.astype(jnp.float32)
        before = dot(marks.astype(jnp.bfloat16), earlier, 1, 0) + so_far
        ranks.append(jnp.sum(marks * before, axis=0, keepdims=True))
        so_far = so_far + jnp.sum(marks, axis=1, keepdims=True)
    rank = jnp.concatenate(ranks, axis=1).astype(jnp.int32)
    plane = ((owners + row_index) % 2) * 2 + rank % 2
    spare = (plane == iota((8, count), 0)).astype(jnp.float32)
    held = jnp.max(jnp.sum(spare, axis=1, keepdims=True) - float(HELD), axis=0, keepdims=True)
    over = jnp.max(rank.astype(jnp.float32), axis=1, keepdims=True) - float(2 * PAIR_SLOTS - 1)
    fits_ref[0] = (jnp.max(jnp.maximum(held, over)) < 0.5).astype(jnp.int32)

    mine = plane == sibling * 2 + half
    block = owners // 2 * PAIR_ROWS
    slot = rank // 2
    chosen = (iota((slots, count), 0) == jnp.where(mine, block + slot, -1)).astype(jnp.bfloat16)
    sent = dot(chosen, rows_ref[...], 1, 0)
    sent = sent * lax.rsqrt(jnp.sum(sent * sent, axis=-1, keepdims=True) + 1e-06)
    high, low = tag_rows(places % owner_rows)
    field = iota((16, count), 0)
    tags = jnp.where(field // 2 == slot, jnp.where(field % 2 == 0, high, low), 0)
    tags = jnp.concatenate([tags, jnp.zeros((LANES - 16, count), jnp.int32)], axis=0)
    tags = tags.astype(jnp.float32).astype(jnp.bfloat16)
    chips = slots // PAIR_ROWS
    sender = iota((chips, count), 0) == jnp.where(mine, owners // 2, -1)
    tags = dot(sender.astype(jnp.bfloat16), tags, 1, 1)
    tags = jnp.broadcast_to(tags[:, None, :], (chips, PAIR_ROWS, LANES)).reshape(slots, LANES)
    wide = features - LANES
    rest = sent[:, wide:]
    line = iota((slots, LANES), 0) % PAIR_ROWS
    for tile in range(PAIR_SLOTS - 1):
        lanes = slice(tile * LANES, (tile + 1) * LANES)
        moved = pltpu.roll(rest, PAIR_SLOTS - tile, 0)
        value = jnp.where(line == PAIR_SLOTS, moved, sent[:, lanes])
        if tile == 0:
            value = jnp.where(line == PAIR_SLOTS + 1, pltpu.roll(rest, 2, 0), value)
        if tile == 1:
            value = jnp.where(line == PAIR_SLOTS + 1, tags, value)
        out_ref[:, lanes] = value.astype(jnp.bfloat16)


def pack_pairs(rows, places, row_index, cent_index, chips, owner_rows):
    count, features = rows.shape
    return pl.pallas_call(
        lambda *refs: pack_pairs_kernel(*refs, owner_rows=owner_rows),
        in_specs=[
            pl.BlockSpec(memory_space=pltpu.SMEM),
            pl.BlockSpec(memory_space=pltpu.SMEM),
            pl.BlockSpec(memory_space=pltpu.VMEM),
            pl.BlockSpec(memory_space=pltpu.VMEM),
        ],
        out_specs=(
            pl.BlockSpec(memory_space=pltpu.VMEM),
            pl.BlockSpec(memory_space=pltpu.SMEM),
        ),
        out_shape=(
            jax.ShapeDtypeStruct((chips * PAIR_ROWS, features - LANES), jnp.bfloat16),
            jax.ShapeDtypeStruct((1,), jnp.int32),
        ),
        name="pack_pairs",
    )(row_index[None], cent_index[None], rows, places[None])


def store_part(out_ref, tags, pieces):
    tag_lines = tags.T[:16].astype(jnp.bfloat16)
    slots = tag_lines.shape[1]
    filled = tag_lines[0:1].astype(jnp.float32) > 0.5
    marks = jnp.broadcast_to(filled.astype(jnp.float32), (16, slots)).astype(jnp.bfloat16)
    before = (iota((slots, slots), 0) < iota((slots, slots), 1)).astype(jnp.bfloat16)
    rank = jnp.where(filled, dot(marks, before, 1, 0)[0:1].astype(jnp.int32), -1)
    picks = (iota((PART, slots), 0) == rank).astype(jnp.bfloat16)
    lines = jnp.concatenate([jnp.zeros((8, PART), jnp.float32), dot(tag_lines[:8], picks, 1, 1)], 0)
    first = 0
    for piece in pieces:
        lanes = slice(first, first + piece.shape[1])
        out_ref[:, lanes] = dot(picks, piece, 1, 0).astype(jnp.bfloat16)
        first = first + piece.shape[1]
    kept = out_ref[PART - 16 :, :PART].astype(jnp.float32)
    out_ref[PART - 16 :, :PART] = (kept + lines).astype(jnp.bfloat16)


def compact_pairs_kernel(got_ref, out_ref):
    slots, wide = got_ref.shape
    line = iota((slots, LANES), 0) % PAIR_ROWS
    lane = iota((slots, LANES), 1)
    rest = jnp.zeros((slots, LANES), jnp.float32)
    placed = jnp.zeros((slots, LANES), jnp.float32)
    tags = got_ref[:, LANES : 2 * LANES].astype(jnp.float32)
    for slot in range(PAIR_SLOTS):
        tile = slot % (PAIR_SLOTS - 1)
        up = PAIR_SLOTS - slot if slot < PAIR_SLOTS - 1 else 2
        value = got_ref[:, tile * LANES : (tile + 1) * LANES].astype(jnp.float32)
        rest = jnp.where(line == slot, pltpu.roll(value, slots - up, 0), rest)
        moved = pltpu.roll(tags, slots - (PAIR_ROWS - 1 - slot), 0)
        moved = pltpu.roll(moved, (LANES - 2 * slot) % LANES, 1) if slot else moved
        placed = jnp.where((line == slot) & (lane < 2), moved, placed)
    store_part(out_ref, placed, [got_ref[...], rest.astype(jnp.bfloat16)])


def pack_kernel(cent_ref, rows_ref, places_ref, out_ref, *, owner_rows):
    normed = normalise(rows_ref[...])
    count, features = normed.shape
    slots = out_ref.shape[0]
    places = places_ref[0]
    owners = places // owner_rows
    earlier = (as_column(owners) == owners) & (iota((count, count), 0) < iota((count, count), 1))
    rank = jnp.sum(earlier.astype(jnp.int32), axis=0, keepdims=True)
    chosen = (iota((slots, count), 0) == owners * SLOTS + rank).astype(jnp.bfloat16)
    high, low = tag_rows(as_column(places % owner_rows))
    lane = iota((count, LANES), 1)
    tags = jnp.where(lane == 0, high, jnp.where(lane == 1, low, 0))
    tags = tags.astype(jnp.float32).astype(jnp.bfloat16)
    out_ref[:, :features] = dot(chosen, normed, 1, 0).astype(jnp.bfloat16)
    out_ref[:, features:] = dot(chosen, tags, 1, 0).astype(jnp.bfloat16)


def pack(rows, places, cent_index, owners, owner_rows, quarters):
    count, features = rows.shape
    quarter = count // quarters
    slots = owners * SLOTS
    return pl.pallas_call(
        lambda *refs: pack_kernel(*refs, owner_rows=owner_rows),
        grid_spec=pltpu.PrefetchScalarGridSpec(
            num_scalar_prefetch=1,
            grid=(1,),
            in_specs=[
                pl.BlockSpec((quarter, features), lambda i, cent: (cent[0], 0)),
                pl.BlockSpec((1, 1, quarter), lambda i, cent: (cent[0], 0, 0)),
            ],
            out_specs=pl.BlockSpec((slots, features + LANES), lambda i, cent: (0, 0)),
        ),
        out_shape=jax.ShapeDtypeStruct((slots, features + LANES), jnp.bfloat16),
        name="pack",
    )(cent_index[None], rows, places.reshape(quarters, 1, quarter))


def compact_kernel(got_ref, out_ref):
    features = out_ref.shape[1]
    tags = got_ref[:, features:].astype(jnp.float32)
    store_part(out_ref, tags, [got_ref[:, :features]])


def compacted(kernel, got, features, name):
    return pl.pallas_call(
        kernel, out_shape=jax.ShapeDtypeStruct((PART, features), jnp.bfloat16), name=name
    )(got)


def decoded(high, low):
    places = jnp.where(high > 0.5, (high - 1.0) * float(TAG_BASE) + low, float(NOWHERE))
    return places.astype(jnp.int32)


def part_tags(part_ref):
    return part_ref[PART - 16 :, : 3 * LANES].astype(jnp.float32)


def place_row(part_ref):
    tags = part_tags(part_ref)
    return decoded(tags[8:9, :PART], tags[9:10, :PART])


def place_column(part_ref):
    tags = part_tags(part_ref).T
    return decoded(tags[:PART, 8:9], tags[:PART, 9:10])


def picked_queries(first_place, count, part_refs):
    queries = 0.0
    for part in part_refs:
        chosen = place_row(part) == first_place + iota((count, PART), 0)
        queries = queries + dot(chosen.astype(jnp.bfloat16), part[...], 1, 0)
    return queries


def compared(best, queries, query_places, starts, part_refs, first_place):
    for part in part_refs:
        column = place_column(part) + first_place
        similarity = dot(part[...], queries, 1, 1)
        allowed = (column >= starts) & (column < query_places)
        masked = jnp.where(allowed, similarity, -1.0)
        best = jnp.maximum(best, jnp.max(masked, axis=0, keepdims=True))
    return best


def early_queries_kernel(first_ref, *refs):
    *part_refs, queries_ref = refs
    queries = picked_queries(first_ref[0], queries_ref.shape[0], part_refs)
    queries_ref[...] = queries.astype(jnp.bfloat16)


def own_kernel(first_ref, starts_ref, early_ref, *refs):
    *part_refs, queries_ref, best_ref = refs
    count = queries_ref.shape[0]
    query_places = first_ref[0] + iota((1, count), 1)
    late = picked_queries(first_ref[0], count, part_refs[-1:])
    queries = (early_ref[...].astype(jnp.float32) + late).astype(jnp.bfloat16)
    queries_ref[...] = queries
    best = jnp.full((1, count), -1.0, jnp.float32)
    best_ref[...] = compared(best, queries, query_places, starts_ref[...], part_refs, 0)


def previous_kernel(first_ref, starts_ref, best_ref, queries_ref, *refs, owner_rows):
    *part_refs, last_ref, out_ref, last_copy, arrived = refs
    copy = pltpu.make_async_copy(last_ref, last_copy, arrived)
    copy.start()
    query_places = first_ref[0] + iota((1, queries_ref.shape[0]), 1)
    queries = queries_ref[...]
    starts = starts_ref[...]
    best = compared(best_ref[...], queries, query_places, starts, part_refs, -owner_rows)
    copy.wait()
    out_ref[...] = compared(best, queries, query_places, starts, [last_copy], -owner_rows)


def whole_call(kernel, out_shape, name, scalar, *arrays, left_there=0, scratch=()):
    here = len(arrays) - left_there
    size = sum(array.size for array in arrays)
    return pl.pallas_call(
        kernel,
        in_specs=[pl.BlockSpec(memory_space=pltpu.SMEM)]
        + [pl.BlockSpec(memory_space=pltpu.VMEM)] * here
        + [pl.BlockSpec(memory_space=pltpu.HBM)] * left_there,
        out_shape=out_shape,
        scratch_shapes=scratch,
        cost_estimate=pl.CostEstimate(
            flops=2 * size * PART, transcendentals=0, bytes_accessed=8 * size
        ),
        name=name,
    )(scalar, *arrays)


def margin_of(embeddings, centroids, positions, slab_starts, slab_ends):
    scores = lax.dot_general(
        normalise(embeddings),
        centroids,
        (((1,), (1,)), ((), ())),
        preferred_element_type=jnp.float32,
    )
    best_sim = jnp.max(scores, axis=1)
    assigned = (slab_starts[None, :] <= positions[:, None]) & (
        positions[:, None] < slab_ends[None, :]
    )
    picked = jnp.sum(jnp.where(assigned, scores, 0.0), axis=1)
    both = jnp.stack([best_sim, picked])
    for both_there in [rotated(both, "cent", by) for by in range(1, lax.axis_size("cent"))]:
        best_sim = jnp.maximum(best_sim, both_there[0])
        picked = picked + both_there[1]
    return best_sim - picked


def on_device(embeddings, centroids, positions, cluster_sizes):
    block_rows, features = embeddings.shape
    row_count = lax.axis_size("rows")
    cent_count = lax.axis_size("cent")
    quarter = block_rows // cent_count
    slab_size = centroids.shape[0]
    row_index = lax.axis_index("rows")
    cent_index = lax.axis_index("cent")
    chips = row_count // 2

    packed, fits = pack_pairs(embeddings, positions, row_index, cent_index, chips, block_rows)

    cluster_ends = jnp.cumsum(cluster_sizes)
    cluster_starts = cluster_ends - cluster_sizes
    slab_ends = lax.dynamic_slice_in_dim(cluster_ends, cent_index * slab_size, slab_size)
    slab_starts = lax.dynamic_slice_in_dim(cluster_starts, cent_index * slab_size, slab_size)

    def by_pairs(packed, embeddings, centroids, positions, slab_starts, slab_ends):
        got = lax.all_to_all(
            packed,
            "rows",
            split_axis=0,
            concat_axis=0,
            tiled=True,
            axis_index_groups=[list(range(core, row_count, 2)) for core in range(2)],
        )
        margin = margin_of(embeddings, centroids, positions, slab_starts, slab_ends)
        return compacted(compact_pairs_kernel, got, features, "compact_pairs"), margin

    def by_quarters(packed, embeddings, centroids, positions, slab_starts, slab_ends):
        packed = pack(embeddings, positions, cent_index, row_count, block_rows, cent_count)
        got = lax.all_to_all(
            packed.reshape(row_count, SLOTS, -1), "rows", split_axis=0, concat_axis=0, tiled=True
        )
        margin = margin_of(embeddings, centroids, positions, slab_starts, slab_ends)
        part = compacted(
            compact_kernel, got.reshape(row_count * SLOTS, -1), features, "compact"
        )
        return from_holders(part, 0, 0), margin

    held, margin = lax.cond(
        fits[0] != 0,
        by_pairs,
        by_quarters,
        packed,
        embeddings,
        centroids,
        positions,
        slab_starts,
        slab_ends,
    )
    base_place = row_index * block_rows
    places = base_place + cent_index * quarter + jnp.arange(quarter, dtype=jnp.int32)
    started = jnp.where(cluster_starts[None, :] <= places[:, None], cluster_starts[None, :], 0)
    starts = (jnp.max(started, axis=1) - base_place)[None, :]

    left = from_holders(held, 1, 0)
    right = from_holders(held, 3, 0)
    previous_here = from_holders(held, 0, 1)
    here = from_holders(held, 0, 0)
    held, left, right, previous_here, here = lax.optimization_barrier(
        (held, left, right, previous_here, here)
    )
    across = from_holders(held, 2, 0)
    previous_left = to_next_owner(left)
    previous_right = to_next_owner(right)

    first = (cent_index * quarter)[None]
    queries_shape = jax.ShapeDtypeStruct((quarter, features), jnp.bfloat16)
    best_shape = jax.ShapeDtypeStruct((1, quarter), jnp.float32)
    early = whole_call(
        early_queries_kernel, queries_shape, "early_queries", first, here, left, right
    )
    across, early, starts = lax.optimization_barrier((across, early, starts))
    previous_across = to_next_owner(across)
    queries, best = whole_call(
        own_kernel, (queries_shape, best_shape), "own", first, starts, early, here, left, right, across
    )
    best = whole_call(
        lambda *refs: previous_kernel(*refs, owner_rows=block_rows),
        best_shape,
        "previous",
        first,
        starts,
        best,
        queries,
        previous_here,
        previous_left,
        previous_right,
        previous_across,
        left_there=1,
        scratch=[pltpu.VMEM((PART, features), jnp.bfloat16), pltpu.SemaphoreType.DMA],
    )
    return (margin, best.reshape(quarter))


def solution(mesh):
    in_specs = (P("rows", None), P("cent", None), P("rows"), P())
    out_specs = (P("rows"), P(("rows", "cent")))
    return jax.shard_map(
        on_device, mesh=mesh, in_specs=in_specs, out_specs=out_specs, check_vma=False
    )
```

```python
import jax
import jax.numpy as jnp
from jax import lax
from jax.experimental import pallas as pl
from jax.experimental.pallas import tpu as pltpu
from jax.sharding import PartitionSpec as P

SLOTS = 4
LANES = 128
TAG_BASE = 32
PAIR_SLOTS = 6
PAIR_ROWS = 8
HELD = 264
PART = 272
NOWHERE = -4096


def rotated(shard, axis, by):
    peers = lax.axis_size(axis)
    return lax.ppermute(shard, axis, [(i, (i + by) % peers) for i in range(peers)])


def to_next_owner(shard):
    row_count = lax.axis_size("rows")
    return lax.ppermute(shard, "rows", [(row, row + 1) for row in range(row_count - 1)])


def from_holders(shard, cent_by, row_by):
    row_count, cent_count = lax.axis_size("rows"), lax.axis_size("cent")
    pairs = []
    for row in range(row_count):
        for cent in range(cent_count):
            target_row = (row ^ (cent // 2)) + row_by
            target_cent = (cent + cent_by) % cent_count
            if target_row < row_count:
                pairs.append((row * cent_count + cent, target_row * cent_count + target_cent))
    return lax.ppermute(shard, ("rows", "cent"), pairs)


def iota(shape, dim):
    return lax.broadcasted_iota(jnp.int32, shape, dim)


def as_column(row):
    size = row.shape[1]
    eye = iota((size, size), 0) == iota((size, size), 1)
    return jnp.sum(jnp.where(eye, row, jnp.zeros_like(row)), axis=1, keepdims=True)


def dot(left, right, left_dim, right_dim):
    return lax.dot_general(
        left, right, (((left_dim,), (right_dim,)), ((), ())), preferred_element_type=jnp.float32
    )


def normalise(rows):
    floats = rows.astype(jnp.float32)
    return (floats * lax.rsqrt(jnp.sum(floats * floats, axis=-1, keepdims=True) + 1e-06)).astype(
        jnp.bfloat16
    )


def tag_rows(local):
    return local // TAG_BASE + 1, local % TAG_BASE


def pack_pairs_kernel(row_ref, cent_ref, rows_ref, places_ref, out_ref, fits_ref, *, owner_rows):
    row_index = row_ref[0]
    sibling = cent_ref[0] // 2
    half = cent_ref[0] % 2
    count, features = rows_ref.shape
    slots = out_ref.shape[0]
    places = places_ref[...]
    owners = places // owner_rows
    owner_count = count // PAIR_ROWS
    step = 256
    earlier = (iota((step, step), 0) < iota((step, step), 1)).astype(jnp.bfloat16)
    so_far = jnp.zeros((owner_count, 1), jnp.float32)
    ranks = []
    for first in range(0, count, step):
        here = iota((owner_count, step), 0) == owners[:, first : first + step]
        marks = here.astype(jnp.float32)
        before = dot(marks.astype(jnp.bfloat16), earlier, 1, 0) + so_far
        ranks.append(jnp.sum(marks * before, axis=0, keepdims=True))
        so_far = so_far + jnp.sum(marks, axis=1, keepdims=True)
    rank = jnp.concatenate(ranks, axis=1).astype(jnp.int32)
    plane = ((owners + row_index) % 2) * 2 + rank % 2
    spare = (plane == iota((8, count), 0)).astype(jnp.float32)
    held = jnp.max(jnp.sum(spare, axis=1, keepdims=True) - float(HELD), axis=0, keepdims=True)
    over = jnp.max(rank.astype(jnp.float32), axis=1, keepdims=True) - float(2 * PAIR_SLOTS - 1)
    fits_ref[0] = (jnp.max(jnp.maximum(held, over)) < 0.5).astype(jnp.int32)

    mine = plane == sibling * 2 + half
    block = owners // 2 * PAIR_ROWS
    slot = rank // 2
    chosen = (iota((slots, count), 0) == jnp.where(mine, block + slot, -1)).astype(jnp.bfloat16)
    sent = dot(chosen, rows_ref[...], 1, 0)
    sent = sent * lax.rsqrt(jnp.sum(sent * sent, axis=-1, keepdims=True) + 1e-06)
    high, low = tag_rows(places % owner_rows)
    field = iota((16, count), 0)
    tags = jnp.where(field // 2 == slot, jnp.where(field % 2 == 0, high, low), 0)
    tags = jnp.concatenate([tags, jnp.zeros((LANES - 16, count), jnp.int32)], axis=0)
    tags = tags.astype(jnp.float32).astype(jnp.bfloat16)
    chips = slots // PAIR_ROWS
    sender = iota((chips, count), 0) == jnp.where(mine, owners // 2, -1)
    tags = dot(sender.astype(jnp.bfloat16), tags, 1, 1)
    tags = jnp.broadcast_to(tags[:, None, :], (chips, PAIR_ROWS, LANES)).reshape(slots, LANES)
    wide = features - LANES
    rest = sent[:, wide:]
    line = iota((slots, LANES), 0) % PAIR_ROWS
    for tile in range(PAIR_SLOTS - 1):
        lanes = slice(tile * LANES, (tile + 1) * LANES)
        moved = pltpu.roll(rest, PAIR_SLOTS - tile, 0)
        value = jnp.where(line == PAIR_SLOTS, moved, sent[:, lanes])
        if tile == 0:
            value = jnp.where(line == PAIR_SLOTS + 1, pltpu.roll(rest, 2, 0), value)
        if tile == 1:
            value = jnp.where(line == PAIR_SLOTS + 1, tags, value)
        out_ref[:, lanes] = value.astype(jnp.bfloat16)


def pack_pairs(rows, places, row_index, cent_index, chips, owner_rows):
    count, features = rows.shape
    return pl.pallas_call(
        lambda *refs: pack_pairs_kernel(*refs, owner_rows=owner_rows),
        in_specs=[
            pl.BlockSpec(memory_space=pltpu.SMEM),
            pl.BlockSpec(memory_space=pltpu.SMEM),
            pl.BlockSpec(memory_space=pltpu.VMEM),
            pl.BlockSpec(memory_space=pltpu.VMEM),
        ],
        out_specs=(
            pl.BlockSpec(memory_space=pltpu.VMEM),
            pl.BlockSpec(memory_space=pltpu.SMEM),
        ),
        out_shape=(
            jax.ShapeDtypeStruct((chips * PAIR_ROWS, features - LANES), jnp.bfloat16),
            jax.ShapeDtypeStruct((1,), jnp.int32),
        ),
        name="pack_pairs",
    )(row_index[None], cent_index[None], rows, places[None])


def store_part(out_ref, tags, pieces):
    tag_lines = tags.T[:16].astype(jnp.bfloat16)
    slots = tag_lines.shape[1]
    filled = tag_lines[0:1].astype(jnp.float32) > 0.5
    marks = jnp.broadcast_to(filled.astype(jnp.float32), (16, slots)).astype(jnp.bfloat16)
    before = (iota((slots, slots), 0) < iota((slots, slots), 1)).astype(jnp.bfloat16)
    rank = jnp.where(filled, dot(marks, before, 1, 0)[0:1].astype(jnp.int32), -1)
    picks = (iota((PART, slots), 0) == rank).astype(jnp.bfloat16)
    lines = jnp.concatenate([jnp.zeros((8, PART), jnp.float32), dot(tag_lines[:8], picks, 1, 1)], 0)
    first = 0
    for piece in pieces:
        lanes = slice(first, first + piece.shape[1])
        out_ref[:, lanes] = dot(picks, piece, 1, 0).astype(jnp.bfloat16)
        first = first + piece.shape[1]
    kept = out_ref[PART - 16 :, :PART].astype(jnp.float32)
    out_ref[PART - 16 :, :PART] = (kept + lines).astype(jnp.bfloat16)


def compact_pairs_kernel(got_ref, out_ref):
    slots, wide = got_ref.shape
    line = iota((slots, LANES), 0) % PAIR_ROWS
    lane = iota((slots, LANES), 1)
    rest = jnp.zeros((slots, LANES), jnp.float32)
    placed = jnp.zeros((slots, LANES), jnp.float32)
    tags = got_ref[:, LANES : 2 * LANES].astype(jnp.float32)
    for slot in range(PAIR_SLOTS):
        tile = slot % (PAIR_SLOTS - 1)
        up = PAIR_SLOTS - slot if slot < PAIR_SLOTS - 1 else 2
        value = got_ref[:, tile * LANES : (tile + 1) * LANES].astype(jnp.float32)
        rest = jnp.where(line == slot, pltpu.roll(value, slots - up, 0), rest)
        moved = pltpu.roll(tags, slots - (PAIR_ROWS - 1 - slot), 0)
        moved = pltpu.roll(moved, (LANES - 2 * slot) % LANES, 1) if slot else moved
        placed = jnp.where((line == slot) & (lane < 2), moved, placed)
    store_part(out_ref, placed, [got_ref[...], rest.astype(jnp.bfloat16)])


def pack_kernel(cent_ref, rows_ref, places_ref, out_ref, *, owner_rows):
    normed = normalise(rows_ref[...])
    count, features = normed.shape
    slots = out_ref.shape[0]
    places = places_ref[0]
    owners = places // owner_rows
    earlier = (as_column(owners) == owners) & (iota((count, count), 0) < iota((count, count), 1))
    rank = jnp.sum(earlier.astype(jnp.int32), axis=0, keepdims=True)
    chosen = (iota((slots, count), 0) == owners * SLOTS + rank).astype(jnp.bfloat16)
    high, low = tag_rows(as_column(places % owner_rows))
    lane = iota((count, LANES), 1)
    tags = jnp.where(lane == 0, high, jnp.where(lane == 1, low, 0))
    tags = tags.astype(jnp.float32).astype(jnp.bfloat16)
    out_ref[:, :features] = dot(chosen, normed, 1, 0).astype(jnp.bfloat16)
    out_ref[:, features:] = dot(chosen, tags, 1, 0).astype(jnp.bfloat16)


def pack(rows, places, cent_index, owners, owner_rows, quarters):
    count, features = rows.shape
    quarter = count // quarters
    slots = owners * SLOTS
    return pl.pallas_call(
        lambda *refs: pack_kernel(*refs, owner_rows=owner_rows),
        grid_spec=pltpu.PrefetchScalarGridSpec(
            num_scalar_prefetch=1,
            grid=(1,),
            in_specs=[
                pl.BlockSpec((quarter, features), lambda i, cent: (cent[0], 0)),
                pl.BlockSpec((1, 1, quarter), lambda i, cent: (cent[0], 0, 0)),
            ],
            out_specs=pl.BlockSpec((slots, features + LANES), lambda i, cent: (0, 0)),
        ),
        out_shape=jax.ShapeDtypeStruct((slots, features + LANES), jnp.bfloat16),
        name="pack",
    )(cent_index[None], rows, places.reshape(quarters, 1, quarter))


def compact_kernel(got_ref, out_ref):
    features = out_ref.shape[1]
    tags = got_ref[:, features:].astype(jnp.float32)
    store_part(out_ref, tags, [got_ref[:, :features]])


def compacted(kernel, got, features, name):
    return pl.pallas_call(
        kernel, out_shape=jax.ShapeDtypeStruct((PART, features), jnp.bfloat16), name=name
    )(got)


def decoded(high, low):
    places = jnp.where(high > 0.5, (high - 1.0) * float(TAG_BASE) + low, float(NOWHERE))
    return places.astype(jnp.int32)


def part_tags(part_ref):
    return part_ref[PART - 16 :, : 3 * LANES].astype(jnp.float32)


def place_row(part_ref):
    tags = part_tags(part_ref)
    return decoded(tags[8:9, :PART], tags[9:10, :PART])


def place_column(part_ref):
    tags = part_tags(part_ref).T
    return decoded(tags[:PART, 8:9], tags[:PART, 9:10])


def start_row(places, start_lines):
    owner_rows = start_lines.shape[1]
    here = (iota((owner_rows, PART), 0) == places).astype(jnp.bfloat16)
    found = dot(start_lines, here, 1, 0)
    return (found[0:1] * 64.0 + found[1:2]).astype(jnp.int32) - owner_rows


def compared(best, queries_ref, places, starts, key_refs):
    for key_ref, key_places in key_refs:
        similarity = dot(key_ref[...], queries_ref[...], 1, 1)
        allowed = (key_places >= starts) & (key_places < places)
        masked = jnp.where(allowed, similarity, -1.0)
        best = jnp.maximum(best, jnp.max(masked, axis=0, keepdims=True))
    return best


def near_kernel(starts_ref, here_ref, left_ref, right_ref, previous_ref, out_ref):
    owner_rows = starts_ref.shape[1]
    starts = starts_ref[...] + owner_rows
    line = iota((16, owner_rows), 0)
    start_lines = jnp.where(line == 0, starts // 64, jnp.where(line == 1, starts % 64, 0))
    start_lines = start_lines.astype(jnp.float32).astype(jnp.bfloat16)
    here = (here_ref, place_column(here_ref))
    left = (left_ref, place_column(left_ref))
    right = (right_ref, place_column(right_ref))
    previous = (previous_ref, place_column(previous_ref) - owner_rows)
    out_ref[...] = jnp.zeros(out_ref.shape, jnp.float32)
    for part, queries_ref, keys in (
        (0, here_ref, (here, left, right, previous)),
        (1, left_ref, (right, previous)),
        (2, right_ref, (previous,)),
    ):
        places = place_row(queries_ref)
        starts = start_row(places, start_lines)
        best = compared(jnp.full((1, PART), -1.0, jnp.float32), queries_ref, places, starts, keys)
        out_ref[8 * part : 8 * part + 1, :PART] = best
        out_ref[8 * part + 1 : 8 * part + 2, :PART] = places.astype(jnp.float32)
        out_ref[8 * part + 2 : 8 * part + 3, :PART] = starts.astype(jnp.float32)


def far_kernel(near_ref, right_ref, previous_left_ref, out_ref):
    owner_rows = out_ref.shape[1]
    lines = near_ref[16:24, :PART]
    places, starts = lines[1:2].astype(jnp.int32), lines[2:3].astype(jnp.int32)
    keys = (previous_left_ref, place_column(previous_left_ref) - owner_rows)
    best_right = compared(lines[0:1], right_ref, places, starts, (keys,))
    best = jnp.full((1, owner_rows), -1.0, jnp.float32)
    lane = iota((PART, owner_rows), 1)
    for part in range(3):
        columns = near_ref[8 * part : 8 * part + 8, :].T
        value = columns[:PART, 0:1]
        if part == 2:
            wide = jnp.broadcast_to(best_right, (8, PART))
            wide = jnp.concatenate([wide, jnp.zeros((8, 3 * LANES - PART), jnp.float32)], axis=1)
            value = wide.T[:PART, 0:1]
        placed = jnp.where(columns[:PART, 1:2].astype(jnp.int32) == lane, value, -1.0)
        best = jnp.maximum(best, jnp.max(placed, axis=0, keepdims=True))
    out_ref[...] = best


def whole_call(kernel, out_shape, name, *arrays):
    size = sum(array.size for array in arrays)
    return pl.pallas_call(
        kernel,
        in_specs=[pl.BlockSpec(memory_space=pltpu.VMEM)] * len(arrays),
        out_shape=out_shape,
        cost_estimate=pl.CostEstimate(
            flops=2 * size * PART, transcendentals=0, bytes_accessed=8 * size
        ),
        name=name,
    )(*arrays)


def margin_of(embeddings, centroids, positions, slab_starts, slab_ends):
    scores = lax.dot_general(
        normalise(embeddings),
        centroids,
        (((1,), (1,)), ((), ())),
        preferred_element_type=jnp.float32,
    )
    best_sim = jnp.max(scores, axis=1)
    assigned = (slab_starts[None, :] <= positions[:, None]) & (
        positions[:, None] < slab_ends[None, :]
    )
    picked = jnp.sum(jnp.where(assigned, scores, 0.0), axis=1)
    both = jnp.stack([best_sim, picked])
    for both_there in [rotated(both, "cent", by) for by in range(1, lax.axis_size("cent"))]:
        best_sim = jnp.maximum(best_sim, both_there[0])
        picked = picked + both_there[1]
    return best_sim - picked


def on_device(embeddings, centroids, positions, cluster_sizes):
    block_rows, features = embeddings.shape
    row_count = lax.axis_size("rows")
    cent_count = lax.axis_size("cent")
    quarter = block_rows // cent_count
    slab_size = centroids.shape[0]
    row_index = lax.axis_index("rows")
    cent_index = lax.axis_index("cent")
    chips = row_count // 2

    packed, fits = pack_pairs(embeddings, positions, row_index, cent_index, chips, block_rows)

    packed, fits, cluster_sizes = lax.optimization_barrier((packed, fits, cluster_sizes))
    cluster_ends = jnp.cumsum(cluster_sizes)
    cluster_starts = cluster_ends - cluster_sizes
    slab_ends = lax.dynamic_slice_in_dim(cluster_ends, cent_index * slab_size, slab_size)
    slab_starts = lax.dynamic_slice_in_dim(cluster_starts, cent_index * slab_size, slab_size)

    def by_pairs(packed, embeddings, centroids, positions, slab_starts, slab_ends):
        got = lax.all_to_all(
            packed,
            "rows",
            split_axis=0,
            concat_axis=0,
            tiled=True,
            axis_index_groups=[list(range(core, row_count, 2)) for core in range(2)],
        )
        margin = margin_of(embeddings, centroids, positions, slab_starts, slab_ends)
        return compacted(compact_pairs_kernel, got, features, "compact_pairs"), margin

    def by_quarters(packed, embeddings, centroids, positions, slab_starts, slab_ends):
        packed = pack(embeddings, positions, cent_index, row_count, block_rows, cent_count)
        got = lax.all_to_all(
            packed.reshape(row_count, SLOTS, -1), "rows", split_axis=0, concat_axis=0, tiled=True
        )
        margin = margin_of(embeddings, centroids, positions, slab_starts, slab_ends)
        part = compacted(
            compact_kernel, got.reshape(row_count * SLOTS, -1), features, "compact"
        )
        return from_holders(part, 0, 0), margin

    held, margin = lax.cond(
        fits[0] != 0,
        by_pairs,
        by_quarters,
        packed,
        embeddings,
        centroids,
        positions,
        slab_starts,
        slab_ends,
    )
    base_place = row_index * block_rows
    places = base_place + jnp.arange(block_rows, dtype=jnp.int32)
    started = jnp.where(cluster_starts[None, :] <= places[:, None], cluster_starts[None, :], 0)
    starts = (jnp.max(started, axis=1) - base_place)[None, :]

    here = from_holders(held, 0, 0)
    previous_here = from_holders(held, 0, 1)
    right = from_holders(held, 3, 0)
    left = from_holders(held, 1, 0)
    here, previous_here, right, left, starts = lax.optimization_barrier(
        (here, previous_here, right, left, starts)
    )
    previous_left = to_next_owner(left)
    near = whole_call(
        near_kernel,
        jax.ShapeDtypeStruct((24, 3 * LANES), jnp.float32),
        "near",
        starts,
        here,
        left,
        right,
        previous_here,
    )
    best = whole_call(
        far_kernel,
        jax.ShapeDtypeStruct((1, block_rows), jnp.float32),
        "far",
        near,
        right,
        previous_left,
    )
    best = lax.all_to_all(
        best.reshape(cent_count, 2, quarter // 2), "cent", split_axis=0, concat_axis=0, tiled=True
    )
    return (margin, jnp.max(best, axis=0).reshape(quarter))


def solution(mesh):
    in_specs = (P("rows", None), P("cent", None), P("rows"), P())
    out_specs = (P("rows"), P(("rows", "cent")))
    return jax.shard_map(
        on_device, mesh=mesh, in_specs=in_specs, out_specs=out_specs, check_vma=False
    )
```

```python
from functools import partial

import jax
import jax.numpy as jnp
from jax import lax
from jax.experimental import pallas as pl
from jax.experimental.pallas import tpu as pltpu
from jax.sharding import PartitionSpec as P

SLOTS = 4
LANES = 128
TAG_BASE = 32
PAIR_SLOTS = (5, 6)
PAIR_ROWS = 8
PAIR_TILES = {5: 4, 6: 5}
HELD = 264
PART = 272
NOWHERE = -4096


def rotated(shard, axis, by):
    peers = lax.axis_size(axis)
    return lax.ppermute(shard, axis, [(i, (i + by) % peers) for i in range(peers)])


def to_next_owner(shard):
    row_count = lax.axis_size("rows")
    return lax.ppermute(shard, "rows", [(row, row + 1) for row in range(row_count - 1)])


def from_holders(shard, cent_by, row_by):
    row_count, cent_count = lax.axis_size("rows"), lax.axis_size("cent")
    pairs = []
    for row in range(row_count):
        for cent in range(cent_count):
            target_row = (row ^ (cent // 2)) + row_by
            target_cent = (cent + cent_by) % cent_count
            if target_row < row_count:
                pairs.append((row * cent_count + cent, target_row * cent_count + target_cent))
    return lax.ppermute(shard, ("rows", "cent"), pairs)


def iota(shape, dim):
    return lax.broadcasted_iota(jnp.int32, shape, dim)


def as_column(row):
    size = row.shape[1]
    eye = iota((size, size), 0) == iota((size, size), 1)
    return jnp.sum(jnp.where(eye, row, jnp.zeros_like(row)), axis=1, keepdims=True)


def dot(left, right, left_dim, right_dim):
    return lax.dot_general(
        left, right, (((left_dim,), (right_dim,)), ((), ())), preferred_element_type=jnp.float32
    )


def normalise(rows):
    floats = rows.astype(jnp.float32)
    return (floats * lax.rsqrt(jnp.sum(floats * floats, axis=-1, keepdims=True) + 1e-06)).astype(
        jnp.bfloat16
    )


def tag_rows(local):
    return local // TAG_BASE + 1, local % TAG_BASE


def spilled(slot, tile, pair_slots, feature_tiles):
    wide = PAIR_TILES[pair_slots]
    cell = slot * (feature_tiles - wide) + tile - wide
    return pair_slots + cell // wide, cell % wide


def pack_pairs_kernel(
    row_ref, cent_ref, rows_ref, places_ref, out_ref, path_ref, *, owner_rows, pair_slots
):
    row_index = row_ref[0]
    sibling = cent_ref[0] // 2
    half = cent_ref[0] % 2
    count, features = rows_ref.shape
    slots = out_ref.shape[0]
    places = places_ref[...]
    owners = places // owner_rows
    owner_count = count // PAIR_ROWS
    step = 256
    earlier = (iota((step, step), 0) < iota((step, step), 1)).astype(jnp.bfloat16)
    so_far = jnp.zeros((owner_count, 1), jnp.float32)
    ranks = []
    for first in range(0, count, step):
        here = iota((owner_count, step), 0) == owners[:, first : first + step]
        marks = here.astype(jnp.float32)
        before = dot(marks.astype(jnp.bfloat16), earlier, 1, 0) + so_far
        ranks.append(jnp.sum(marks * before, axis=0, keepdims=True))
        so_far = so_far + jnp.sum(marks, axis=1, keepdims=True)
    rank = jnp.concatenate(ranks, axis=1).astype(jnp.int32)
    plane = ((owners + row_index) % 2) * 2 + rank % 2
    counts = jnp.sum((plane == iota((8, count), 0)).astype(jnp.float32), axis=1, keepdims=True)
    crowded = jnp.max(counts) > HELD
    most = jnp.max(rank.astype(jnp.float32))
    path = jnp.int32(0)
    for slots_there in PAIR_SLOTS:
        path = path + (crowded | (most >= 2 * slots_there)).astype(jnp.int32)
    path_ref[0] = path

    mine = plane == sibling * 2 + half
    block = owners // 2 * PAIR_ROWS
    slot = rank // 2
    chosen = (iota((slots, count), 0) == jnp.where(mine, block + slot, -1)).astype(jnp.bfloat16)
    sent = dot(chosen, rows_ref[...], 1, 0)
    sent = sent * lax.rsqrt(jnp.sum(sent * sent, axis=-1, keepdims=True) + 1e-06)
    high, low = tag_rows(places % owner_rows)
    field = iota((16, count), 0)
    tags = jnp.where(field // 2 == slot, jnp.where(field % 2 == 0, high, low), 0)
    tags = jnp.concatenate([tags, jnp.zeros((LANES - 16, count), jnp.int32)], axis=0)
    tags = tags.astype(jnp.float32).astype(jnp.bfloat16)
    chips = slots // PAIR_ROWS
    sender = iota((chips, count), 0) == jnp.where(mine, owners // 2, -1)
    tags = dot(sender.astype(jnp.bfloat16), tags, 1, 1)
    tags = jnp.broadcast_to(tags[:, None, :], (chips, PAIR_ROWS, LANES)).reshape(slots, LANES)
    wide = PAIR_TILES[pair_slots]
    tiles = features // LANES
    line = iota((slots, LANES), 0) % PAIR_ROWS
    values = [sent[:, tile * LANES : (tile + 1) * LANES] for tile in range(tiles)]
    for slot in range(pair_slots):
        for tile in range(wide, tiles):
            row, lanes = spilled(slot, tile, pair_slots, tiles)
            moved = pltpu.roll(values[tile], row - slot, 0)
            values[lanes] = jnp.where(line == row, moved, values[lanes])
    row, lanes = spilled(pair_slots, wide, pair_slots, tiles)
    values[lanes] = jnp.where(line == row, tags, values[lanes])
    for tile in range(wide):
        out_ref[:, tile * LANES : (tile + 1) * LANES] = values[tile].astype(jnp.bfloat16)


def pack_pairs(rows, places, row_index, cent_index, chips, owner_rows, pair_slots):
    count, features = rows.shape
    return pl.pallas_call(
        lambda *refs: pack_pairs_kernel(*refs, owner_rows=owner_rows, pair_slots=pair_slots),
        in_specs=[
            pl.BlockSpec(memory_space=pltpu.SMEM),
            pl.BlockSpec(memory_space=pltpu.SMEM),
            pl.BlockSpec(memory_space=pltpu.VMEM),
            pl.BlockSpec(memory_space=pltpu.VMEM),
        ],
        out_specs=(
            pl.BlockSpec(memory_space=pltpu.VMEM),
            pl.BlockSpec(memory_space=pltpu.SMEM),
        ),
        out_shape=(
            jax.ShapeDtypeStruct((chips * PAIR_ROWS, PAIR_TILES[pair_slots] * LANES), jnp.bfloat16),
            jax.ShapeDtypeStruct((1,), jnp.int32),
        ),
        name=f"pack_pairs_{pair_slots}",
    )(row_index[None], cent_index[None], rows, places[None])


def store_part(out_ref, tags, pieces):
    tag_lines = tags.T[:16].astype(jnp.bfloat16)
    slots = tag_lines.shape[1]
    filled = tag_lines[0:1].astype(jnp.float32) > 0.5
    marks = jnp.broadcast_to(filled.astype(jnp.float32), (16, slots)).astype(jnp.bfloat16)
    before = (iota((slots, slots), 0) < iota((slots, slots), 1)).astype(jnp.bfloat16)
    rank = jnp.where(filled, dot(marks, before, 1, 0)[0:1].astype(jnp.int32), -1)
    picks = (iota((PART, slots), 0) == rank).astype(jnp.bfloat16)
    lines = jnp.concatenate([jnp.zeros((8, PART), jnp.float32), dot(tag_lines[:8], picks, 1, 1)], 0)
    first = 0
    for piece in pieces:
        lanes = slice(first, first + piece.shape[1])
        out_ref[:, lanes] = dot(picks, piece, 1, 0).astype(jnp.bfloat16)
        first = first + piece.shape[1]
    kept = out_ref[PART - 16 :, :PART].astype(jnp.float32)
    out_ref[PART - 16 :, :PART] = (kept + lines).astype(jnp.bfloat16)


def compact_pairs_kernel(got_ref, out_ref, *, pair_slots):
    slots = got_ref.shape[0]
    wide = PAIR_TILES[pair_slots]
    tiles = out_ref.shape[1] // LANES
    line = iota((slots, LANES), 0) % PAIR_ROWS
    lane = iota((slots, LANES), 1)
    values = [
        got_ref[:, tile * LANES : (tile + 1) * LANES].astype(jnp.float32) for tile in range(wide)
    ]
    tag_row, lanes = spilled(pair_slots, wide, pair_slots, tiles)
    tags = values[lanes]
    placed = jnp.zeros((slots, LANES), jnp.float32)
    rest = [jnp.zeros((slots, LANES), jnp.float32)] * (tiles - wide)
    for slot in range(pair_slots):
        for tile in range(wide, tiles):
            row, lanes = spilled(slot, tile, pair_slots, tiles)
            moved = pltpu.roll(values[lanes], slots - (row - slot), 0)
            rest[tile - wide] = jnp.where(line == slot, moved, rest[tile - wide])
        moved = pltpu.roll(tags, slots - (tag_row - slot), 0)
        moved = pltpu.roll(moved, (LANES - 2 * slot) % LANES, 1) if slot else moved
        placed = jnp.where((line == slot) & (lane < 2), moved, placed)
    store_part(out_ref, placed, [got_ref[...]] + [tile.astype(jnp.bfloat16) for tile in rest])


def pack_kernel(cent_ref, rows_ref, places_ref, out_ref, *, owner_rows):
    normed = normalise(rows_ref[...])
    count, features = normed.shape
    slots = out_ref.shape[0]
    places = places_ref[0]
    owners = places // owner_rows
    earlier = (as_column(owners) == owners) & (iota((count, count), 0) < iota((count, count), 1))
    rank = jnp.sum(earlier.astype(jnp.int32), axis=0, keepdims=True)
    chosen = (iota((slots, count), 0) == owners * SLOTS + rank).astype(jnp.bfloat16)
    high, low = tag_rows(as_column(places % owner_rows))
    lane = iota((count, LANES), 1)
    tags = jnp.where(lane == 0, high, jnp.where(lane == 1, low, 0))
    tags = tags.astype(jnp.float32).astype(jnp.bfloat16)
    out_ref[:, :features] = dot(chosen, normed, 1, 0).astype(jnp.bfloat16)
    out_ref[:, features:] = dot(chosen, tags, 1, 0).astype(jnp.bfloat16)


def pack(rows, places, cent_index, owners, owner_rows, quarters):
    count, features = rows.shape
    quarter = count // quarters
    slots = owners * SLOTS
    return pl.pallas_call(
        lambda *refs: pack_kernel(*refs, owner_rows=owner_rows),
        grid_spec=pltpu.PrefetchScalarGridSpec(
            num_scalar_prefetch=1,
            grid=(1,),
            in_specs=[
                pl.BlockSpec((quarter, features), lambda i, cent: (cent[0], 0)),
                pl.BlockSpec((1, 1, quarter), lambda i, cent: (cent[0], 0, 0)),
            ],
            out_specs=pl.BlockSpec((slots, features + LANES), lambda i, cent: (0, 0)),
        ),
        out_shape=jax.ShapeDtypeStruct((slots, features + LANES), jnp.bfloat16),
        name="pack",
    )(cent_index[None], rows, places.reshape(quarters, 1, quarter))


def compact_kernel(got_ref, out_ref):
    features = out_ref.shape[1]
    tags = got_ref[:, features:].astype(jnp.float32)
    store_part(out_ref, tags, [got_ref[:, :features]])


def compacted(kernel, got, features, name):
    return pl.pallas_call(
        kernel, out_shape=jax.ShapeDtypeStruct((PART, features), jnp.bfloat16), name=name
    )(got)


def decoded(high, low):
    places = jnp.where(high > 0.5, (high - 1.0) * float(TAG_BASE) + low, float(NOWHERE))
    return places.astype(jnp.int32)


def part_tags(part_ref):
    return part_ref[PART - 16 :, : 3 * LANES].astype(jnp.float32)


def place_row(part_ref):
    tags = part_tags(part_ref)
    return decoded(tags[8:9, :PART], tags[9:10, :PART])


def place_column(part_ref):
    tags = part_tags(part_ref).T
    return decoded(tags[:PART, 8:9], tags[:PART, 9:10])


def start_row(places, start_lines):
    owner_rows = start_lines.shape[1]
    here = (iota((owner_rows, PART), 0) == places).astype(jnp.bfloat16)
    found = dot(start_lines, here, 1, 0)
    return (found[0:1] * 64.0 + found[1:2]).astype(jnp.int32) - owner_rows


def compared(best, queries_ref, places, starts, key_refs):
    for key_ref, key_places in key_refs:
        similarity = dot(key_ref[...], queries_ref[...], 1, 1)
        allowed = (key_places >= starts) & (key_places < places)
        masked = jnp.where(allowed, similarity, -1.0)
        best = jnp.maximum(best, jnp.max(masked, axis=0, keepdims=True))
    return best


def at_places(best, places, values):
    lines = jnp.concatenate([values, places.astype(jnp.float32)], axis=0)
    lines = jnp.concatenate([lines, jnp.zeros((6, PART), jnp.float32)], axis=0)
    spare = jnp.zeros((8, 3 * LANES - PART), jnp.float32)
    columns = jnp.concatenate([lines, spare], axis=1).T
    owner_rows = best.shape[1]
    there = columns[:PART, 1:2].astype(jnp.int32) == iota((PART, owner_rows), 1)
    placed = jnp.where(there, columns[:PART, 0:1], -1.0)
    return jnp.maximum(best, jnp.max(placed, axis=0, keepdims=True))


def near_kernel(starts_ref, here_ref, left_ref, right_ref, previous_ref, best_ref, right_lines_ref):
    owner_rows = starts_ref.shape[1]
    starts = starts_ref[...] + owner_rows
    line = iota((16, owner_rows), 0)
    start_lines = jnp.where(line == 0, starts // 64, jnp.where(line == 1, starts % 64, 0))
    start_lines = start_lines.astype(jnp.float32).astype(jnp.bfloat16)
    here = (here_ref, place_column(here_ref))
    left = (left_ref, place_column(left_ref))
    right = (right_ref, place_column(right_ref))
    previous = (previous_ref, place_column(previous_ref) - owner_rows)
    placed = jnp.full((1, owner_rows), -1.0, jnp.float32)
    for queries_ref, keys in (
        (here_ref, (here, left, right, previous)),
        (left_ref, (right, previous)),
        (right_ref, (previous,)),
    ):
        places = place_row(queries_ref)
        starts = start_row(places, start_lines)
        best = compared(jnp.full((1, PART), -1.0, jnp.float32), queries_ref, places, starts, keys)
        if queries_ref is not right_ref:
            placed = at_places(placed, places, best)
    best_ref[...] = placed
    right_lines_ref[0:1, :] = best
    right_lines_ref[1:2, :] = places.astype(jnp.float32)
    right_lines_ref[2:3, :] = starts.astype(jnp.float32)


def far_kernel(best_ref, right_lines_ref, right_ref, previous_left_ref, out_ref):
    owner_rows = out_ref.shape[1]
    places = right_lines_ref[1:2, :].astype(jnp.int32)
    starts = right_lines_ref[2:3, :].astype(jnp.int32)
    keys = (previous_left_ref, place_column(previous_left_ref) - owner_rows)
    best = compared(right_lines_ref[0:1, :], right_ref, places, starts, (keys,))
    out_ref[...] = at_places(best_ref[...], places, best)


def whole_call(kernel, out_shape, name, *arrays):
    size = sum(array.size for array in arrays)
    return pl.pallas_call(
        kernel,
        in_specs=[pl.BlockSpec(memory_space=pltpu.VMEM)] * len(arrays),
        out_shape=out_shape,
        cost_estimate=pl.CostEstimate(
            flops=2 * size * PART, transcendentals=0, bytes_accessed=8 * size
        ),
        name=name,
    )(*arrays)


def margin_of(embeddings, centroids, positions, slab_starts, slab_ends):
    scores = lax.dot_general(
        normalise(embeddings),
        centroids,
        (((1,), (1,)), ((), ())),
        preferred_element_type=jnp.float32,
    )
    best_sim = jnp.max(scores, axis=1)
    assigned = (slab_starts[None, :] <= positions[:, None]) & (
        positions[:, None] < slab_ends[None, :]
    )
    picked = jnp.sum(jnp.where(assigned, scores, 0.0), axis=1)
    both = jnp.stack([best_sim, picked])
    for both_there in [rotated(both, "cent", by) for by in range(1, lax.axis_size("cent"))]:
        best_sim = jnp.maximum(best_sim, both_there[0])
        picked = picked + both_there[1]
    return best_sim - picked


def on_device(embeddings, centroids, positions, cluster_sizes):
    block_rows, features = embeddings.shape
    row_count = lax.axis_size("rows")
    cent_count = lax.axis_size("cent")
    quarter = block_rows // cent_count
    slab_size = centroids.shape[0]
    row_index = lax.axis_index("rows")
    cent_index = lax.axis_index("cent")
    chips = row_count // 2

    def packed_in(pair_slots, embeddings, positions):
        return pack_pairs(
            embeddings, positions, row_index, cent_index, chips, block_rows, pair_slots
        )

    packed, path = packed_in(PAIR_SLOTS[0], embeddings, positions)

    packed, path, cluster_sizes = lax.optimization_barrier((packed, path, cluster_sizes))
    cluster_ends = jnp.cumsum(cluster_sizes)
    cluster_starts = cluster_ends - cluster_sizes
    slab_ends = lax.dynamic_slice_in_dim(cluster_ends, cent_index * slab_size, slab_size)
    slab_starts = lax.dynamic_slice_in_dim(cluster_starts, cent_index * slab_size, slab_size)

    def by_pairs(pair_slots, packed, embeddings, centroids, positions, slab_starts, slab_ends):
        if pair_slots != PAIR_SLOTS[0]:
            packed, _ = packed_in(pair_slots, embeddings, positions)
        got = lax.all_to_all(
            packed,
            "rows",
            split_axis=0,
            concat_axis=0,
            tiled=True,
            axis_index_groups=[list(range(core, row_count, 2)) for core in range(2)],
        )
        margin = margin_of(embeddings, centroids, positions, slab_starts, slab_ends)
        kernel = partial(compact_pairs_kernel, pair_slots=pair_slots)
        return compacted(kernel, got, features, f"compact_pairs_{pair_slots}"), margin

    def by_quarters(packed, embeddings, centroids, positions, slab_starts, slab_ends):
        packed = pack(embeddings, positions, cent_index, row_count, block_rows, cent_count)
        got = lax.all_to_all(
            packed.reshape(row_count, SLOTS, -1), "rows", split_axis=0, concat_axis=0, tiled=True
        )
        margin = margin_of(embeddings, centroids, positions, slab_starts, slab_ends)
        part = compacted(
            compact_kernel, got.reshape(row_count * SLOTS, -1), features, "compact"
        )
        return from_holders(part, 0, 0), margin

    held, margin = lax.switch(
        path[0],
        [partial(by_pairs, pair_slots) for pair_slots in PAIR_SLOTS] + [by_quarters],
        packed,
        embeddings,
        centroids,
        positions,
        slab_starts,
        slab_ends,
    )
    base_place = row_index * block_rows
    places = base_place + jnp.arange(block_rows, dtype=jnp.int32)
    started = jnp.where(cluster_starts[None, :] <= places[:, None], cluster_starts[None, :], 0)
    starts = (jnp.max(started, axis=1) - base_place)[None, :]

    here = from_holders(held, 0, 0)
    previous_here = from_holders(held, 0, 1)
    right = from_holders(held, 3, 0)
    left = from_holders(held, 1, 0)
    here, previous_here, right, left, starts = lax.optimization_barrier(
        (here, previous_here, right, left, starts)
    )
    previous_left = to_next_owner(left)
    best_shape = jax.ShapeDtypeStruct((1, block_rows), jnp.float32)
    best, right_lines = whole_call(
        near_kernel,
        (best_shape, jax.ShapeDtypeStruct((3, PART), jnp.float32)),
        "near",
        starts,
        here,
        left,
        right,
        previous_here,
    )
    best = whole_call(
        far_kernel,
        best_shape,
        "far",
        best,
        right_lines,
        right,
        previous_left,
    )
    best = lax.all_to_all(
        best.reshape(cent_count, 2, quarter // 2), "cent", split_axis=0, concat_axis=0, tiled=True
    )
    return (margin, jnp.max(best, axis=0).reshape(quarter))


def solution(mesh):
    in_specs = (P("rows", None), P("cent", None), P("rows"), P())
    out_specs = (P("rows"), P(("rows", "cent")))
    return jax.shard_map(
        on_device, mesh=mesh, in_specs=in_specs, out_specs=out_specs, check_vma=False
    )
```

```python
from functools import partial

import jax
import jax.numpy as jnp
from jax import lax
from jax.experimental import pallas as pl
from jax.experimental.pallas import tpu as pltpu
from jax.sharding import PartitionSpec as P

SLOTS = 4
LANES = 128
TAG_BASE = 32
PAIR_SLOTS = (5, 6)
PAIR_ROWS = 8
PAIR_TILES = {5: 4, 6: 5}
HELD = 264
PART = 272
NOWHERE = -4096


def rotated(shard, axis, by):
    peers = lax.axis_size(axis)
    return lax.ppermute(shard, axis, [(i, (i + by) % peers) for i in range(peers)])


def to_next_owner(shard):
    row_count = lax.axis_size("rows")
    return lax.ppermute(shard, "rows", [(row, row + 1) for row in range(row_count - 1)])


def from_holders(shard, cent_by, row_by):
    row_count, cent_count = lax.axis_size("rows"), lax.axis_size("cent")
    pairs = []
    for row in range(row_count):
        for cent in range(cent_count):
            target_row = (row ^ (cent // 2)) + row_by
            target_cent = (cent + cent_by) % cent_count
            if target_row < row_count:
                pairs.append((row * cent_count + cent, target_row * cent_count + target_cent))
    return lax.ppermute(shard, ("rows", "cent"), pairs)


def iota(shape, dim):
    return lax.broadcasted_iota(jnp.int32, shape, dim)


def as_column(row):
    size = row.shape[1]
    eye = iota((size, size), 0) == iota((size, size), 1)
    return jnp.sum(jnp.where(eye, row, jnp.zeros_like(row)), axis=1, keepdims=True)


def dot(left, right, left_dim, right_dim):
    return lax.dot_general(
        left, right, (((left_dim,), (right_dim,)), ((), ())), preferred_element_type=jnp.float32
    )


def normalise(rows):
    floats = rows.astype(jnp.float32)
    return (floats * lax.rsqrt(jnp.sum(floats * floats, axis=-1, keepdims=True) + 1e-06)).astype(
        jnp.bfloat16
    )


def tag_rows(local):
    return local // TAG_BASE + 1, local % TAG_BASE


def spilled(slot, tile, pair_slots, feature_tiles):
    wide = PAIR_TILES[pair_slots]
    cell = slot * (feature_tiles - wide) + tile - wide
    return pair_slots + cell // wide, cell % wide


def pack_pairs_kernel(
    row_ref, cent_ref, rows_ref, places_ref, out_ref, path_ref, *, owner_rows, pair_slots
):
    row_index = row_ref[0]
    sibling = cent_ref[0] // 2
    half = cent_ref[0] % 2
    count, features = rows_ref.shape
    slots = out_ref.shape[0]
    places = places_ref[...]
    owners = places // owner_rows
    owner_count = count // PAIR_ROWS
    step = 256
    earlier = (iota((step, step), 0) < iota((step, step), 1)).astype(jnp.bfloat16)
    so_far = jnp.zeros((owner_count, 1), jnp.float32)
    ranks = []
    for first in range(0, count, step):
        here = iota((owner_count, step), 0) == owners[:, first : first + step]
        marks = here.astype(jnp.float32)
        before = dot(marks.astype(jnp.bfloat16), earlier, 1, 0) + so_far
        ranks.append(jnp.sum(marks * before, axis=0, keepdims=True))
        so_far = so_far + jnp.sum(marks, axis=1, keepdims=True)
    rank = jnp.concatenate(ranks, axis=1).astype(jnp.int32)
    plane = ((owners + row_index) % 2) * 2 + rank % 2
    counts = jnp.sum((plane == iota((8, count), 0)).astype(jnp.float32), axis=1, keepdims=True)
    crowded = jnp.max(counts) > HELD
    most = jnp.max(rank.astype(jnp.float32))
    path = jnp.int32(0)
    for slots_there in PAIR_SLOTS:
        path = path + (crowded | (most >= 2 * slots_there)).astype(jnp.int32)
    path_ref[0] = path

    mine = plane == sibling * 2 + half
    block = owners // 2 * PAIR_ROWS
    slot = rank // 2
    chosen = (iota((slots, count), 0) == jnp.where(mine, block + slot, -1)).astype(jnp.bfloat16)
    sent = dot(chosen, rows_ref[...], 1, 0)
    sent = sent * lax.rsqrt(jnp.sum(sent * sent, axis=-1, keepdims=True) + 1e-06)
    high, low = tag_rows(places % owner_rows)
    field = iota((16, count), 0)
    tags = jnp.where(field // 2 == slot, jnp.where(field % 2 == 0, high, low), 0)
    tags = jnp.concatenate([tags, jnp.zeros((LANES - 16, count), jnp.int32)], axis=0)
    tags = tags.astype(jnp.float32).astype(jnp.bfloat16)
    chips = slots // PAIR_ROWS
    sender = iota((chips, count), 0) == jnp.where(mine, owners // 2, -1)
    tags = dot(sender.astype(jnp.bfloat16), tags, 1, 1)
    tags = jnp.broadcast_to(tags[:, None, :], (chips, PAIR_ROWS, LANES)).reshape(slots, LANES)
    wide = PAIR_TILES[pair_slots]
    tiles = features // LANES
    line = iota((slots, LANES), 0) % PAIR_ROWS
    values = [sent[:, tile * LANES : (tile + 1) * LANES] for tile in range(tiles)]
    for slot in range(pair_slots):
        for tile in range(wide, tiles):
            row, lanes = spilled(slot, tile, pair_slots, tiles)
            moved = pltpu.roll(values[tile], row - slot, 0)
            values[lanes] = jnp.where(line == row, moved, values[lanes])
    row, lanes = spilled(pair_slots, wide, pair_slots, tiles)
    values[lanes] = jnp.where(line == row, tags, values[lanes])
    for tile in range(wide):
        out_ref[:, tile * LANES : (tile + 1) * LANES] = values[tile].astype(jnp.bfloat16)


def pack_pairs(rows, places, row_index, cent_index, chips, owner_rows, pair_slots):
    count, features = rows.shape
    return pl.pallas_call(
        lambda *refs: pack_pairs_kernel(*refs, owner_rows=owner_rows, pair_slots=pair_slots),
        in_specs=[
            pl.BlockSpec(memory_space=pltpu.SMEM),
            pl.BlockSpec(memory_space=pltpu.SMEM),
            pl.BlockSpec(memory_space=pltpu.VMEM),
            pl.BlockSpec(memory_space=pltpu.VMEM),
        ],
        out_specs=(
            pl.BlockSpec(memory_space=pltpu.VMEM),
            pl.BlockSpec(memory_space=pltpu.SMEM),
        ),
        out_shape=(
            pltpu.VMEM((chips * PAIR_ROWS, PAIR_TILES[pair_slots] * LANES), jnp.bfloat16),
            jax.ShapeDtypeStruct((1,), jnp.int32),
        ),
        name=f"pack_pairs_{pair_slots}",
    )(row_index[None], cent_index[None], rows, places[None])


def store_part(out_ref, tags, pieces):
    tag_lines = tags.T[:16].astype(jnp.bfloat16)
    slots = tag_lines.shape[1]
    filled = tag_lines[0:1].astype(jnp.float32) > 0.5
    marks = jnp.broadcast_to(filled.astype(jnp.float32), (16, slots)).astype(jnp.bfloat16)
    before = (iota((slots, slots), 0) < iota((slots, slots), 1)).astype(jnp.bfloat16)
    rank = jnp.where(filled, dot(marks, before, 1, 0)[0:1].astype(jnp.int32), -1)
    picks = (iota((PART, slots), 0) == rank).astype(jnp.bfloat16)
    lines = jnp.concatenate([jnp.zeros((8, PART), jnp.float32), dot(tag_lines[:8], picks, 1, 1)], 0)
    first = 0
    for piece in pieces:
        lanes = slice(first, first + piece.shape[1])
        out_ref[:, lanes] = dot(picks, piece, 1, 0).astype(jnp.bfloat16)
        first = first + piece.shape[1]
    kept = out_ref[PART - 16 :, :PART].astype(jnp.float32)
    out_ref[PART - 16 :, :PART] = (kept + lines).astype(jnp.bfloat16)


def compact_pairs_kernel(got_ref, out_ref, *, pair_slots):
    slots = got_ref.shape[0]
    wide = PAIR_TILES[pair_slots]
    tiles = out_ref.shape[1] // LANES
    line = iota((slots, LANES), 0) % PAIR_ROWS
    lane = iota((slots, LANES), 1)
    values = [
        got_ref[:, tile * LANES : (tile + 1) * LANES].astype(jnp.float32) for tile in range(wide)
    ]
    tag_row, lanes = spilled(pair_slots, wide, pair_slots, tiles)
    tags = values[lanes]
    placed = jnp.zeros((slots, LANES), jnp.float32)
    rest = [jnp.zeros((slots, LANES), jnp.float32)] * (tiles - wide)
    for slot in range(pair_slots):
        for tile in range(wide, tiles):
            row, lanes = spilled(slot, tile, pair_slots, tiles)
            moved = pltpu.roll(values[lanes], slots - (row - slot), 0)
            rest[tile - wide] = jnp.where(line == slot, moved, rest[tile - wide])
        moved = pltpu.roll(tags, slots - (tag_row - slot), 0)
        moved = pltpu.roll(moved, (LANES - 2 * slot) % LANES, 1) if slot else moved
        placed = jnp.where((line == slot) & (lane < 2), moved, placed)
    rest = jnp.concatenate(rest, axis=1).astype(jnp.bfloat16)
    store_part(out_ref, placed, [got_ref[...], rest])


def pack_kernel(cent_ref, rows_ref, places_ref, out_ref, *, owner_rows):
    normed = normalise(rows_ref[...])
    count, features = normed.shape
    slots = out_ref.shape[0]
    places = places_ref[0]
    owners = places // owner_rows
    earlier = (as_column(owners) == owners) & (iota((count, count), 0) < iota((count, count), 1))
    rank = jnp.sum(earlier.astype(jnp.int32), axis=0, keepdims=True)
    chosen = (iota((slots, count), 0) == owners * SLOTS + rank).astype(jnp.bfloat16)
    high, low = tag_rows(as_column(places % owner_rows))
    lane = iota((count, LANES), 1)
    tags = jnp.where(lane == 0, high, jnp.where(lane == 1, low, 0))
    tags = tags.astype(jnp.float32).astype(jnp.bfloat16)
    out_ref[:, :features] = dot(chosen, normed, 1, 0).astype(jnp.bfloat16)
    out_ref[:, features:] = dot(chosen, tags, 1, 0).astype(jnp.bfloat16)


def pack(rows, places, cent_index, owners, owner_rows, quarters):
    count, features = rows.shape
    quarter = count // quarters
    slots = owners * SLOTS
    return pl.pallas_call(
        lambda *refs: pack_kernel(*refs, owner_rows=owner_rows),
        grid_spec=pltpu.PrefetchScalarGridSpec(
            num_scalar_prefetch=1,
            grid=(1,),
            in_specs=[
                pl.BlockSpec((quarter, features), lambda i, cent: (cent[0], 0)),
                pl.BlockSpec((1, 1, quarter), lambda i, cent: (cent[0], 0, 0)),
            ],
            out_specs=pl.BlockSpec((slots, features + LANES), lambda i, cent: (0, 0)),
        ),
        out_shape=jax.ShapeDtypeStruct((slots, features + LANES), jnp.bfloat16),
        name="pack",
    )(cent_index[None], rows, places.reshape(quarters, 1, quarter))


def compact_kernel(got_ref, out_ref):
    features = out_ref.shape[1]
    tags = got_ref[:, features:].astype(jnp.float32)
    store_part(out_ref, tags, [got_ref[:, :features]])


def on_chip(array):
    return pltpu.with_memory_space_constraint(array, pltpu.VMEM)


def compacted(kernel, got, features, name):
    return pl.pallas_call(
        kernel,
        in_specs=[pl.BlockSpec(memory_space=pltpu.VMEM)],
        out_shape=pltpu.VMEM((PART, features), jnp.bfloat16),
        name=name,
    )(on_chip(got))


def decoded(high, low):
    places = jnp.where(high > 0.5, (high - 1.0) * float(TAG_BASE) + low, float(NOWHERE))
    return places.astype(jnp.int32)


def part_tags(part_ref):
    return part_ref[PART - 16 :, : 3 * LANES].astype(jnp.float32)


def place_row(part_ref):
    tags = part_tags(part_ref)
    return decoded(tags[8:9, :PART], tags[9:10, :PART])


def place_column(part_ref):
    tags = part_tags(part_ref).T
    return decoded(tags[:PART, 8:9], tags[:PART, 9:10])


def start_row(places, start_lines):
    owner_rows = start_lines.shape[1]
    here = (iota((owner_rows, PART), 0) == places).astype(jnp.bfloat16)
    found = dot(start_lines, here, 1, 0)
    return (found[0:1] * 64.0 + found[1:2]).astype(jnp.int32) - owner_rows


def compared(best, queries_ref, places, starts, key_refs):
    for key_ref, key_places in key_refs:
        similarity = dot(key_ref[...], queries_ref[...], 1, 1)
        allowed = (key_places >= starts) & (key_places < places)
        masked = jnp.where(allowed, similarity, -1.0)
        best = jnp.maximum(best, jnp.max(masked, axis=0, keepdims=True))
    return best


def at_places(best, places, values):
    lines = jnp.concatenate([values, places.astype(jnp.float32)], axis=0)
    lines = jnp.concatenate([lines, jnp.zeros((6, PART), jnp.float32)], axis=0)
    spare = jnp.zeros((8, 3 * LANES - PART), jnp.float32)
    columns = jnp.concatenate([lines, spare], axis=1).T
    owner_rows = best.shape[1]
    there = columns[:PART, 1:2].astype(jnp.int32) == iota((PART, owner_rows), 1)
    placed = jnp.where(there, columns[:PART, 0:1], -1.0)
    return jnp.maximum(best, jnp.max(placed, axis=0, keepdims=True))


def near_kernel(starts_ref, here_ref, left_ref, right_ref, previous_ref, best_ref, right_lines_ref):
    owner_rows = starts_ref.shape[1]
    starts = starts_ref[...] + owner_rows
    line = iota((16, owner_rows), 0)
    start_lines = jnp.where(line == 0, starts // 64, jnp.where(line == 1, starts % 64, 0))
    start_lines = start_lines.astype(jnp.float32).astype(jnp.bfloat16)
    here = (here_ref, place_column(here_ref))
    left = (left_ref, place_column(left_ref))
    right = (right_ref, place_column(right_ref))
    previous = (previous_ref, place_column(previous_ref) - owner_rows)
    placed = jnp.full((1, owner_rows), -1.0, jnp.float32)
    for queries_ref, keys in (
        (here_ref, (here, left, right, previous)),
        (left_ref, (right, previous)),
        (right_ref, (previous,)),
    ):
        places = place_row(queries_ref)
        starts = start_row(places, start_lines)
        best = compared(jnp.full((1, PART), -1.0, jnp.float32), queries_ref, places, starts, keys)
        if queries_ref is not right_ref:
            placed = at_places(placed, places, best)
    best_ref[...] = placed
    right_lines_ref[0:1, :] = best
    right_lines_ref[1:2, :] = places.astype(jnp.float32)
    right_lines_ref[2:3, :] = starts.astype(jnp.float32)


def far_kernel(best_ref, right_lines_ref, right_ref, previous_left_ref, out_ref):
    owner_rows = out_ref.shape[1]
    places = right_lines_ref[1:2, :].astype(jnp.int32)
    starts = right_lines_ref[2:3, :].astype(jnp.int32)
    keys = (previous_left_ref, place_column(previous_left_ref) - owner_rows)
    best = compared(right_lines_ref[0:1, :], right_ref, places, starts, (keys,))
    out_ref[...] = at_places(best_ref[...], places, best)


def whole_call(kernel, out_shape, name, *arrays):
    size = sum(array.size for array in arrays)
    return pl.pallas_call(
        kernel,
        in_specs=[pl.BlockSpec(memory_space=pltpu.VMEM)] * len(arrays),
        out_shape=out_shape,
        cost_estimate=pl.CostEstimate(
            flops=2 * size * PART, transcendentals=0, bytes_accessed=8 * size
        ),
        name=name,
    )(*[on_chip(array) for array in arrays])


def margin_of(embeddings, centroids, positions, slab_starts, slab_ends):
    scores = lax.dot_general(
        normalise(embeddings),
        centroids,
        (((1,), (1,)), ((), ())),
        preferred_element_type=jnp.float32,
    )
    best_sim = jnp.max(scores, axis=1)
    assigned = (slab_starts[None, :] <= positions[:, None]) & (
        positions[:, None] < slab_ends[None, :]
    )
    picked = jnp.sum(jnp.where(assigned, scores, 0.0), axis=1)
    both = jnp.stack([best_sim, picked])
    for both_there in [rotated(both, "cent", by) for by in range(1, lax.axis_size("cent"))]:
        best_sim = jnp.maximum(best_sim, both_there[0])
        picked = picked + both_there[1]
    return best_sim - picked


def on_device(embeddings, centroids, positions, cluster_sizes):
    block_rows, features = embeddings.shape
    row_count = lax.axis_size("rows")
    cent_count = lax.axis_size("cent")
    quarter = block_rows // cent_count
    slab_size = centroids.shape[0]
    row_index = lax.axis_index("rows")
    cent_index = lax.axis_index("cent")
    chips = row_count // 2

    def packed_in(pair_slots, embeddings, positions):
        return pack_pairs(
            embeddings, positions, row_index, cent_index, chips, block_rows, pair_slots
        )

    packed, path = packed_in(PAIR_SLOTS[0], embeddings, positions)

    packed, path, cluster_sizes = lax.optimization_barrier((packed, path, cluster_sizes))
    cluster_ends = jnp.cumsum(cluster_sizes)
    cluster_starts = cluster_ends - cluster_sizes
    slab_ends = lax.dynamic_slice_in_dim(cluster_ends, cent_index * slab_size, slab_size)
    slab_starts = lax.dynamic_slice_in_dim(cluster_starts, cent_index * slab_size, slab_size)

    def by_pairs(pair_slots, packed, embeddings, centroids, positions, slab_starts, slab_ends):
        if pair_slots != PAIR_SLOTS[0]:
            packed, _ = packed_in(pair_slots, embeddings, positions)
        got = lax.all_to_all(
            packed,
            "rows",
            split_axis=0,
            concat_axis=0,
            tiled=True,
            axis_index_groups=[list(range(core, row_count, 2)) for core in range(2)],
        )
        margin = margin_of(embeddings, centroids, positions, slab_starts, slab_ends)
        kernel = partial(compact_pairs_kernel, pair_slots=pair_slots)
        return compacted(kernel, got, features, f"compact_pairs_{pair_slots}"), margin

    def by_quarters(packed, embeddings, centroids, positions, slab_starts, slab_ends):
        packed = pack(embeddings, positions, cent_index, row_count, block_rows, cent_count)
        got = lax.all_to_all(
            packed.reshape(row_count, SLOTS, -1), "rows", split_axis=0, concat_axis=0, tiled=True
        )
        margin = margin_of(embeddings, centroids, positions, slab_starts, slab_ends)
        part = compacted(
            compact_kernel, got.reshape(row_count * SLOTS, -1), features, "compact"
        )
        return from_holders(part, 0, 0), margin

    held, margin = lax.switch(
        path[0],
        [partial(by_pairs, pair_slots) for pair_slots in PAIR_SLOTS] + [by_quarters],
        packed,
        embeddings,
        centroids,
        positions,
        slab_starts,
        slab_ends,
    )
    base_place = row_index * block_rows
    places = base_place + jnp.arange(block_rows, dtype=jnp.int32)
    started = jnp.where(cluster_starts[None, :] <= places[:, None], cluster_starts[None, :], 0)
    starts = (jnp.max(started, axis=1) - base_place)[None, :]

    here = from_holders(held, 0, 0)
    previous_here = from_holders(held, 0, 1)
    right = from_holders(held, 3, 0)
    left = from_holders(held, 1, 0)
    here, previous_here, right, left, starts = lax.optimization_barrier(
        (here, previous_here, right, left, starts)
    )
    previous_left = to_next_owner(left)
    best_shape = pltpu.VMEM((1, block_rows), jnp.float32)
    best, right_lines = whole_call(
        near_kernel,
        (best_shape, pltpu.VMEM((3, PART), jnp.float32)),
        "near",
        starts,
        here,
        left,
        right,
        previous_here,
    )
    best = whole_call(
        far_kernel,
        best_shape,
        "far",
        best,
        right_lines,
        right,
        previous_left,
    )
    best = lax.all_to_all(
        best.reshape(cent_count, 2, quarter // 2), "cent", split_axis=0, concat_axis=0, tiled=True
    )
    return (margin, jnp.max(best, axis=0).reshape(quarter))


def solution(mesh):
    in_specs = (P("rows", None), P("cent", None), P("rows"), P())
    out_specs = (P("rows"), P(("rows", "cent")))
    return jax.shard_map(
        on_device, mesh=mesh, in_specs=in_specs, out_specs=out_specs, check_vma=False
    )
```

```python
from functools import partial

import jax
import jax.numpy as jnp
from jax import lax
from jax.experimental import pallas as pl
from jax.experimental.pallas import tpu as pltpu
from jax.sharding import PartitionSpec as P

SLOTS = 4
LANES = 128
TAG_BASE = 32
PAIR_SLOTS = (5, 6)
PAIR_ROWS = 8
PAIR_TILES = {5: 4, 6: 5}
HELD = 264
PART = 272
NOWHERE = -4096


def rotated(shard, axis, by):
    peers = lax.axis_size(axis)
    return lax.ppermute(shard, axis, [(i, (i + by) % peers) for i in range(peers)])


def to_next_owner(shard):
    row_count = lax.axis_size("rows")
    return lax.ppermute(shard, "rows", [(row, row + 1) for row in range(row_count - 1)])


def from_holders(shard, cent_by, row_by):
    row_count, cent_count = lax.axis_size("rows"), lax.axis_size("cent")
    pairs = []
    for row in range(row_count):
        for cent in range(cent_count):
            target_row = (row ^ (cent // 2)) + row_by
            target_cent = (cent + cent_by) % cent_count
            if target_row < row_count:
                pairs.append((row * cent_count + cent, target_row * cent_count + target_cent))
    return lax.ppermute(shard, ("rows", "cent"), pairs)


def iota(shape, dim):
    return lax.broadcasted_iota(jnp.int32, shape, dim)


def as_column(row):
    size = row.shape[1]
    eye = iota((size, size), 0) == iota((size, size), 1)
    return jnp.sum(jnp.where(eye, row, jnp.zeros_like(row)), axis=1, keepdims=True)


def dot(left, right, left_dim, right_dim):
    return lax.dot_general(
        left, right, (((left_dim,), (right_dim,)), ((), ())), preferred_element_type=jnp.float32
    )


def normalise(rows):
    floats = rows.astype(jnp.float32)
    return (floats * lax.rsqrt(jnp.sum(floats * floats, axis=-1, keepdims=True) + 1e-06)).astype(
        jnp.bfloat16
    )


def tag_rows(local):
    return local // TAG_BASE + 1, local % TAG_BASE


def spilled(slot, tile, pair_slots, feature_tiles):
    wide = PAIR_TILES[pair_slots]
    cell = slot * (feature_tiles - wide) + tile - wide
    return pair_slots + cell // wide, cell % wide


def pack_pairs_kernel(
    row_ref, cent_ref, rows_ref, places_ref, out_ref, path_ref, *, owner_rows, pair_slots
):
    row_index = row_ref[0]
    sibling = cent_ref[0] // 2
    half = cent_ref[0] % 2
    count, features = rows_ref.shape
    slots = out_ref.shape[0]
    places = places_ref[...]
    owners = places // owner_rows
    owner_count = count // PAIR_ROWS
    step = 256
    earlier = (iota((step, step), 0) < iota((step, step), 1)).astype(jnp.bfloat16)
    so_far = jnp.zeros((owner_count, 1), jnp.float32)
    ranks = []
    for first in range(0, count, step):
        here = iota((owner_count, step), 0) == owners[:, first : first + step]
        marks = here.astype(jnp.float32)
        before = dot(marks.astype(jnp.bfloat16), earlier, 1, 0) + so_far
        ranks.append(jnp.sum(marks * before, axis=0, keepdims=True))
        so_far = so_far + jnp.sum(marks, axis=1, keepdims=True)
    rank = jnp.concatenate(ranks, axis=1).astype(jnp.int32)
    plane = ((owners + row_index) % 2) * 2 + rank % 2
    counts = jnp.sum((plane == iota((8, count), 0)).astype(jnp.float32), axis=1, keepdims=True)
    crowded = jnp.max(counts) > HELD
    most = jnp.max(rank.astype(jnp.float32))
    path = jnp.int32(0)
    for slots_there in PAIR_SLOTS:
        path = path + (crowded | (most >= 2 * slots_there)).astype(jnp.int32)
    path_ref[0] = path

    mine = plane == sibling * 2 + half
    block = owners // 2 * PAIR_ROWS
    slot = rank // 2
    chosen = (iota((slots, count), 0) == jnp.where(mine, block + slot, -1)).astype(jnp.bfloat16)
    sent = dot(chosen, rows_ref[...], 1, 0)
    sent = sent * lax.rsqrt(jnp.sum(sent * sent, axis=-1, keepdims=True) + 1e-06)
    high, low = tag_rows(places % owner_rows)
    field = iota((16, count), 0)
    tags = jnp.where(field // 2 == slot, jnp.where(field % 2 == 0, high, low), 0)
    tags = jnp.concatenate([tags, jnp.zeros((LANES - 16, count), jnp.int32)], axis=0)
    tags = tags.astype(jnp.float32).astype(jnp.bfloat16)
    chips = slots // PAIR_ROWS
    sender = iota((chips, count), 0) == jnp.where(mine, owners // 2, -1)
    tags = dot(sender.astype(jnp.bfloat16), tags, 1, 1)
    tags = jnp.broadcast_to(tags[:, None, :], (chips, PAIR_ROWS, LANES)).reshape(slots, LANES)
    wide = PAIR_TILES[pair_slots]
    tiles = features // LANES
    line = iota((slots, LANES), 0) % PAIR_ROWS
    values = [sent[:, tile * LANES : (tile + 1) * LANES] for tile in range(tiles)]
    for slot in range(pair_slots):
        for tile in range(wide, tiles):
            row, lanes = spilled(slot, tile, pair_slots, tiles)
            moved = pltpu.roll(values[tile], row - slot, 0)
            values[lanes] = jnp.where(line == row, moved, values[lanes])
    row, lanes = spilled(pair_slots, wide, pair_slots, tiles)
    values[lanes] = jnp.where(line == row, tags, values[lanes])
    for tile in range(wide):
        out_ref[:, tile * LANES : (tile + 1) * LANES] = values[tile].astype(jnp.bfloat16)


def pack_pairs(rows, places, row_index, cent_index, chips, owner_rows, pair_slots):
    count, features = rows.shape
    return pl.pallas_call(
        lambda *refs: pack_pairs_kernel(*refs, owner_rows=owner_rows, pair_slots=pair_slots),
        in_specs=[
            pl.BlockSpec(memory_space=pltpu.SMEM),
            pl.BlockSpec(memory_space=pltpu.SMEM),
            pl.BlockSpec(memory_space=pltpu.VMEM),
            pl.BlockSpec(memory_space=pltpu.VMEM),
        ],
        out_specs=(
            pl.BlockSpec(memory_space=pltpu.VMEM),
            pl.BlockSpec(memory_space=pltpu.SMEM),
        ),
        out_shape=(
            pltpu.VMEM((chips * PAIR_ROWS, PAIR_TILES[pair_slots] * LANES), jnp.bfloat16),
            jax.ShapeDtypeStruct((1,), jnp.int32),
        ),
        name=f"pack_pairs_{pair_slots}",
    )(row_index[None], cent_index[None], rows, places[None])


def store_part(out_ref, tags, pieces):
    tag_lines = tags.T[:16].astype(jnp.bfloat16)
    slots = tag_lines.shape[1]
    filled = tag_lines[0:1].astype(jnp.float32) > 0.5
    marks = jnp.broadcast_to(filled.astype(jnp.float32), (16, slots)).astype(jnp.bfloat16)
    before = (iota((slots, slots), 0) < iota((slots, slots), 1)).astype(jnp.bfloat16)
    rank = jnp.where(filled, dot(marks, before, 1, 0)[0:1].astype(jnp.int32), -1)
    picks = (iota((PART, slots), 0) == rank).astype(jnp.bfloat16)
    lines = jnp.concatenate([jnp.zeros((8, PART), jnp.float32), dot(tag_lines[:8], picks, 1, 1)], 0)
    first = 0
    for piece in pieces:
        lanes = slice(first, first + piece.shape[1])
        out_ref[:, lanes] = dot(picks, piece, 1, 0).astype(jnp.bfloat16)
        first = first + piece.shape[1]
    kept = out_ref[PART - 16 :, :PART].astype(jnp.float32)
    out_ref[PART - 16 :, :PART] = (kept + lines).astype(jnp.bfloat16)


def compact_pairs_kernel(got_ref, out_ref, *, pair_slots):
    slots = got_ref.shape[0]
    wide = PAIR_TILES[pair_slots]
    tiles = out_ref.shape[1] // LANES
    line = iota((slots, LANES), 0) % PAIR_ROWS
    lane = iota((slots, LANES), 1)
    values = [
        got_ref[:, tile * LANES : (tile + 1) * LANES].astype(jnp.float32) for tile in range(wide)
    ]
    tag_row, lanes = spilled(pair_slots, wide, pair_slots, tiles)
    tags = values[lanes]
    placed = jnp.zeros((slots, LANES), jnp.float32)
    rest = [jnp.zeros((slots, LANES), jnp.float32)] * (tiles - wide)
    for slot in range(pair_slots):
        for tile in range(wide, tiles):
            row, lanes = spilled(slot, tile, pair_slots, tiles)
            moved = pltpu.roll(values[lanes], slots - (row - slot), 0)
            rest[tile - wide] = jnp.where(line == slot, moved, rest[tile - wide])
        moved = pltpu.roll(tags, slots - (tag_row - slot), 0)
        moved = pltpu.roll(moved, (LANES - 2 * slot) % LANES, 1) if slot else moved
        placed = jnp.where((line == slot) & (lane < 2), moved, placed)
    rest = jnp.concatenate(rest, axis=1).astype(jnp.bfloat16)
    store_part(out_ref, placed, [got_ref[...], rest])


def pack_kernel(cent_ref, rows_ref, places_ref, out_ref, *, owner_rows):
    normed = normalise(rows_ref[...])
    count, features = normed.shape
    slots = out_ref.shape[0]
    places = places_ref[0]
    owners = places // owner_rows
    earlier = (as_column(owners) == owners) & (iota((count, count), 0) < iota((count, count), 1))
    rank = jnp.sum(earlier.astype(jnp.int32), axis=0, keepdims=True)
    chosen = (iota((slots, count), 0) == owners * SLOTS + rank).astype(jnp.bfloat16)
    high, low = tag_rows(as_column(places % owner_rows))
    lane = iota((count, LANES), 1)
    tags = jnp.where(lane == 0, high, jnp.where(lane == 1, low, 0))
    tags = tags.astype(jnp.float32).astype(jnp.bfloat16)
    out_ref[:, :features] = dot(chosen, normed, 1, 0).astype(jnp.bfloat16)
    out_ref[:, features:] = dot(chosen, tags, 1, 0).astype(jnp.bfloat16)


def pack(rows, places, cent_index, owners, owner_rows, quarters):
    count, features = rows.shape
    quarter = count // quarters
    slots = owners * SLOTS
    return pl.pallas_call(
        lambda *refs: pack_kernel(*refs, owner_rows=owner_rows),
        grid_spec=pltpu.PrefetchScalarGridSpec(
            num_scalar_prefetch=1,
            grid=(1,),
            in_specs=[
                pl.BlockSpec((quarter, features), lambda i, cent: (cent[0], 0)),
                pl.BlockSpec((1, 1, quarter), lambda i, cent: (cent[0], 0, 0)),
            ],
            out_specs=pl.BlockSpec((slots, features + LANES), lambda i, cent: (0, 0)),
        ),
        out_shape=jax.ShapeDtypeStruct((slots, features + LANES), jnp.bfloat16),
        name="pack",
    )(cent_index[None], rows, places.reshape(quarters, 1, quarter))


def compact_kernel(got_ref, out_ref):
    features = out_ref.shape[1]
    tags = got_ref[:, features:].astype(jnp.float32)
    store_part(out_ref, tags, [got_ref[:, :features]])


def on_chip(array):
    return pltpu.with_memory_space_constraint(array, pltpu.VMEM)


def compacted(kernel, got, features, name):
    return pl.pallas_call(
        kernel,
        in_specs=[pl.BlockSpec(memory_space=pltpu.VMEM)],
        out_shape=pltpu.VMEM((PART, features), jnp.bfloat16),
        name=name,
    )(on_chip(got))


def decoded(high, low):
    places = jnp.where(high > 0.5, (high - 1.0) * float(TAG_BASE) + low, float(NOWHERE))
    return places.astype(jnp.int32)


def part_tags(part_ref):
    return part_ref[PART - 16 :, : 3 * LANES].astype(jnp.float32)


def place_row(part_ref):
    tags = part_tags(part_ref)
    return decoded(tags[8:9, :PART], tags[9:10, :PART])


def place_column(part_ref):
    tags = part_tags(part_ref).T
    return decoded(tags[:PART, 8:9], tags[:PART, 9:10])


def start_row(places, start_lines):
    owner_rows = start_lines.shape[1]
    here = (iota((owner_rows, PART), 0) == places).astype(jnp.bfloat16)
    found = dot(start_lines, here, 1, 0)
    return (found[0:1] * 64.0 + found[1:2]).astype(jnp.int32) - owner_rows


def compared(best, queries_ref, places, starts, key_refs):
    for key_ref, key_places in key_refs:
        similarity = dot(key_ref[...], queries_ref[...], 1, 1)
        allowed = (key_places >= starts) & (key_places < places)
        masked = jnp.where(allowed, similarity, -1.0)
        best = jnp.maximum(best, jnp.max(masked, axis=0, keepdims=True))
    return best


def at_places(best, places, values):
    lines = jnp.concatenate([values, places.astype(jnp.float32)], axis=0)
    lines = jnp.concatenate([lines, jnp.zeros((6, PART), jnp.float32)], axis=0)
    spare = jnp.zeros((8, 3 * LANES - PART), jnp.float32)
    columns = jnp.concatenate([lines, spare], axis=1).T
    owner_rows = best.shape[1]
    there = columns[:PART, 1:2].astype(jnp.int32) == iota((PART, owner_rows), 1)
    placed = jnp.where(there, columns[:PART, 0:1], -1.0)
    return jnp.maximum(best, jnp.max(placed, axis=0, keepdims=True))


def near_kernel(starts_ref, here_ref, left_ref, right_ref, previous_ref, best_ref, right_lines_ref):
    owner_rows = starts_ref.shape[1]
    starts = starts_ref[...] + owner_rows
    line = iota((16, owner_rows), 0)
    start_lines = jnp.where(line == 0, starts // 64, jnp.where(line == 1, starts % 64, 0))
    start_lines = start_lines.astype(jnp.float32).astype(jnp.bfloat16)
    here = (here_ref, place_column(here_ref))
    left = (left_ref, place_column(left_ref))
    right = (right_ref, place_column(right_ref))
    previous = (previous_ref, place_column(previous_ref) - owner_rows)
    placed = jnp.full((1, owner_rows), -1.0, jnp.float32)
    for queries_ref, keys in (
        (here_ref, (here, left, right, previous)),
        (left_ref, (right, previous)),
        (right_ref, (previous,)),
    ):
        places = place_row(queries_ref)
        starts = start_row(places, start_lines)
        best = compared(jnp.full((1, PART), -1.0, jnp.float32), queries_ref, places, starts, keys)
        if queries_ref is not right_ref:
            placed = at_places(placed, places, best)
    best_ref[...] = placed
    right_lines_ref[0:1, :] = best
    right_lines_ref[1:2, :] = places.astype(jnp.float32)
    right_lines_ref[2:3, :] = starts.astype(jnp.float32)


def far_kernel(best_ref, right_lines_ref, right_ref, previous_left_ref, out_ref):
    owner_rows = out_ref.shape[1]
    places = right_lines_ref[1:2, :].astype(jnp.int32)
    starts = right_lines_ref[2:3, :].astype(jnp.int32)
    keys = (previous_left_ref, place_column(previous_left_ref) - owner_rows)
    best = compared(right_lines_ref[0:1, :], right_ref, places, starts, (keys,))
    out_ref[...] = at_places(best_ref[...], places, best)


def whole_call(kernel, out_shape, name, *arrays):
    size = sum(array.size for array in arrays)
    return pl.pallas_call(
        kernel,
        in_specs=[pl.BlockSpec(memory_space=pltpu.VMEM)] * len(arrays),
        out_shape=out_shape,
        cost_estimate=pl.CostEstimate(
            flops=2 * size * PART, transcendentals=0, bytes_accessed=8 * size
        ),
        name=name,
    )(*[on_chip(array) for array in arrays])


def margin_of(embeddings, centroids, positions, slab_starts, slab_ends):
    scores = lax.dot_general(
        normalise(embeddings),
        centroids,
        (((1,), (1,)), ((), ())),
        preferred_element_type=jnp.float32,
    )
    best_sim = jnp.max(scores, axis=1)
    assigned = (slab_starts[None, :] <= positions[:, None]) & (
        positions[:, None] < slab_ends[None, :]
    )
    picked = jnp.sum(jnp.where(assigned, scores, 0.0), axis=1)
    both = jnp.stack([best_sim, picked])
    for both_there in [rotated(both, "cent", by) for by in range(1, lax.axis_size("cent"))]:
        best_sim = jnp.maximum(best_sim, both_there[0])
        picked = picked + both_there[1]
    return best_sim - picked


def on_device(embeddings, centroids, positions, cluster_sizes):
    block_rows, features = embeddings.shape
    row_count = lax.axis_size("rows")
    cent_count = lax.axis_size("cent")
    quarter = block_rows // cent_count
    slab_size = centroids.shape[0]
    row_index = lax.axis_index("rows")
    cent_index = lax.axis_index("cent")
    chips = row_count // 2

    def packed_in(pair_slots, embeddings, positions):
        return pack_pairs(
            embeddings, positions, row_index, cent_index, chips, block_rows, pair_slots
        )

    packed, path = packed_in(PAIR_SLOTS[0], embeddings, positions)

    packed, path, cluster_sizes = lax.optimization_barrier((packed, path, cluster_sizes))
    cluster_ends = jnp.cumsum(cluster_sizes)
    cluster_starts = cluster_ends - cluster_sizes
    slab_ends = lax.dynamic_slice_in_dim(cluster_ends, cent_index * slab_size, slab_size)
    slab_starts = lax.dynamic_slice_in_dim(cluster_starts, cent_index * slab_size, slab_size)

    def by_pairs(pair_slots, packed, embeddings, centroids, positions, slab_starts, slab_ends):
        if pair_slots != PAIR_SLOTS[0]:
            packed, _ = packed_in(pair_slots, embeddings, positions)
        got = lax.all_to_all(
            packed,
            "rows",
            split_axis=0,
            concat_axis=0,
            tiled=True,
            axis_index_groups=[list(range(core, row_count, 2)) for core in range(2)],
        )
        margin = margin_of(embeddings, centroids, positions, slab_starts, slab_ends)
        kernel = partial(compact_pairs_kernel, pair_slots=pair_slots)
        return compacted(kernel, got, features, f"compact_pairs_{pair_slots}"), margin

    def by_quarters(packed, embeddings, centroids, positions, slab_starts, slab_ends):
        packed = pack(embeddings, positions, cent_index, row_count, block_rows, cent_count)
        got = lax.all_to_all(
            packed.reshape(row_count, SLOTS, -1), "rows", split_axis=0, concat_axis=0, tiled=True
        )
        margin = margin_of(embeddings, centroids, positions, slab_starts, slab_ends)
        part = compacted(
            compact_kernel, got.reshape(row_count * SLOTS, -1), features, "compact"
        )
        return from_holders(part, 0, 0), margin

    held, margin = lax.switch(
        path[0],
        [partial(by_pairs, pair_slots) for pair_slots in PAIR_SLOTS] + [by_quarters],
        packed,
        embeddings,
        centroids,
        positions,
        slab_starts,
        slab_ends,
    )
    base_place = row_index * block_rows
    places = base_place + jnp.arange(block_rows, dtype=jnp.int32)
    started = jnp.where(cluster_starts[None, :] <= places[:, None], cluster_starts[None, :], 0)
    starts = (jnp.max(started, axis=1) - base_place)[None, :]

    right = from_holders(held, 3, 0)
    left = from_holders(held, 1, 0)
    held, starts = lax.optimization_barrier((held, starts))
    here = from_holders(held, 0, 0)
    previous_here = from_holders(held, 0, 1)
    right, left, starts = lax.optimization_barrier((right, left, starts))
    previous_left = to_next_owner(left)
    best_shape = pltpu.VMEM((1, block_rows), jnp.float32)
    best, right_lines = whole_call(
        near_kernel,
        (best_shape, pltpu.VMEM((3, PART), jnp.float32)),
        "near",
        starts,
        here,
        left,
        right,
        previous_here,
    )
    best = whole_call(
        far_kernel,
        best_shape,
        "far",
        best,
        right_lines,
        right,
        previous_left,
    )
    best = lax.all_to_all(
        best.reshape(cent_count, 2, quarter // 2), "cent", split_axis=0, concat_axis=0, tiled=True
    )
    return (margin, jnp.max(best, axis=0).reshape(quarter))


def solution(mesh):
    in_specs = (P("rows", None), P("cent", None), P("rows"), P())
    out_specs = (P("rows"), P(("rows", "cent")))
    return jax.shard_map(
        on_device, mesh=mesh, in_specs=in_specs, out_specs=out_specs, check_vma=False
    )
```

```python
from functools import partial

import jax
import jax.numpy as jnp
from jax import lax
from jax.experimental import pallas as pl
from jax.experimental.pallas import tpu as pltpu
from jax.sharding import PartitionSpec as P

SLOTS = 4
LANES = 128
TAG_BASE = 32
PAIR_SLOTS = (5, 6)
PAIR_ROWS = 8
PAIR_TILES = {5: 4, 6: 5}
HELD = 264
PART = 272
NOWHERE = -4096


def rotated(shard, axis, by):
    peers = lax.axis_size(axis)
    return lax.ppermute(shard, axis, [(i, (i + by) % peers) for i in range(peers)])


def to_next_owner(shard):
    row_count = lax.axis_size("rows")
    return lax.ppermute(shard, "rows", [(row, row + 1) for row in range(row_count - 1)])


def from_holders(shard, cent_by, row_by):
    row_count, cent_count = lax.axis_size("rows"), lax.axis_size("cent")
    pairs = []
    for row in range(row_count):
        for cent in range(cent_count):
            target_row = (row ^ (cent // 2)) + row_by
            target_cent = (cent + cent_by) % cent_count
            if target_row < row_count:
                pairs.append((row * cent_count + cent, target_row * cent_count + target_cent))
    return lax.ppermute(shard, ("rows", "cent"), pairs)


def iota(shape, dim):
    return lax.broadcasted_iota(jnp.int32, shape, dim)


def as_column(row):
    size = row.shape[1]
    eye = iota((size, size), 0) == iota((size, size), 1)
    return jnp.sum(jnp.where(eye, row, jnp.zeros_like(row)), axis=1, keepdims=True)


def dot(left, right, left_dim, right_dim):
    return lax.dot_general(
        left, right, (((left_dim,), (right_dim,)), ((), ())), preferred_element_type=jnp.float32
    )


def normalise(rows):
    floats = rows.astype(jnp.float32)
    return (floats * lax.rsqrt(jnp.sum(floats * floats, axis=-1, keepdims=True) + 1e-06)).astype(
        jnp.bfloat16
    )


def tag_rows(local):
    return local // TAG_BASE + 1, local % TAG_BASE


def spilled(slot, tile, pair_slots, feature_tiles):
    wide = PAIR_TILES[pair_slots]
    cell = slot * (feature_tiles - wide) + tile - wide
    return pair_slots + cell // wide, cell % wide


def pack_pairs_kernel(
    row_ref, cent_ref, rows_ref, places_ref, out_ref, path_ref, *, owner_rows, pair_slots
):
    row_index = row_ref[0]
    sibling = cent_ref[0] // 2
    half = cent_ref[0] % 2
    count, features = rows_ref.shape
    slots = out_ref.shape[0]
    places = places_ref[...]
    owners = places // owner_rows
    owner_count = count // PAIR_ROWS
    step = 256
    earlier = (iota((step, step), 0) < iota((step, step), 1)).astype(jnp.bfloat16)
    so_far = jnp.zeros((owner_count, 1), jnp.float32)
    ranks = []
    for first in range(0, count, step):
        here = iota((owner_count, step), 0) == owners[:, first : first + step]
        marks = here.astype(jnp.float32)
        before = dot(marks.astype(jnp.bfloat16), earlier, 1, 0) + so_far
        ranks.append(jnp.sum(marks * before, axis=0, keepdims=True))
        so_far = so_far + jnp.sum(marks, axis=1, keepdims=True)
    rank = jnp.concatenate(ranks, axis=1).astype(jnp.int32)
    plane = ((owners + row_index) % 2) * 2 + rank % 2
    counts = jnp.sum((plane == iota((8, count), 0)).astype(jnp.float32), axis=1, keepdims=True)
    crowded = jnp.max(counts) > HELD
    most = jnp.max(rank.astype(jnp.float32))
    path = jnp.int32(0)
    for slots_there in PAIR_SLOTS:
        path = path + (crowded | (most >= 2 * slots_there)).astype(jnp.int32)
    path_ref[0] = path

    mine = plane == sibling * 2 + half
    block = owners // 2 * PAIR_ROWS
    slot = rank // 2
    chosen = (iota((slots, count), 0) == jnp.where(mine, block + slot, -1)).astype(jnp.bfloat16)
    sent = dot(chosen, rows_ref[...], 1, 0)
    sent = sent * lax.rsqrt(jnp.sum(sent * sent, axis=-1, keepdims=True) + 1e-06)
    high, low = tag_rows(places % owner_rows)
    field = iota((16, count), 0)
    tags = jnp.where(field // 2 == slot, jnp.where(field % 2 == 0, high, low), 0)
    tags = jnp.concatenate([tags, jnp.zeros((LANES - 16, count), jnp.int32)], axis=0)
    tags = tags.astype(jnp.float32).astype(jnp.bfloat16)
    chips = slots // PAIR_ROWS
    sender = iota((chips, count), 0) == jnp.where(mine, owners // 2, -1)
    tags = dot(sender.astype(jnp.bfloat16), tags, 1, 1)
    tags = jnp.broadcast_to(tags[:, None, :], (chips, PAIR_ROWS, LANES)).reshape(slots, LANES)
    wide = PAIR_TILES[pair_slots]
    tiles = features // LANES
    line = iota((slots, LANES), 0) % PAIR_ROWS
    values = [sent[:, tile * LANES : (tile + 1) * LANES] for tile in range(tiles)]
    for slot in range(pair_slots):
        for tile in range(wide, tiles):
            row, lanes = spilled(slot, tile, pair_slots, tiles)
            moved = pltpu.roll(values[tile], row - slot, 0)
            values[lanes] = jnp.where(line == row, moved, values[lanes])
    row, lanes = spilled(pair_slots, wide, pair_slots, tiles)
    values[lanes] = jnp.where(line == row, tags, values[lanes])
    for tile in range(wide):
        out_ref[:, tile * LANES : (tile + 1) * LANES] = values[tile].astype(jnp.bfloat16)


def pack_pairs(rows, places, row_index, cent_index, chips, owner_rows, pair_slots):
    count, features = rows.shape
    return pl.pallas_call(
        lambda *refs: pack_pairs_kernel(*refs, owner_rows=owner_rows, pair_slots=pair_slots),
        in_specs=[
            pl.BlockSpec(memory_space=pltpu.SMEM),
            pl.BlockSpec(memory_space=pltpu.SMEM),
            pl.BlockSpec(memory_space=pltpu.VMEM),
            pl.BlockSpec(memory_space=pltpu.VMEM),
        ],
        out_specs=(
            pl.BlockSpec(memory_space=pltpu.VMEM),
            pl.BlockSpec(memory_space=pltpu.SMEM),
        ),
        out_shape=(
            pltpu.VMEM((chips * PAIR_ROWS, PAIR_TILES[pair_slots] * LANES), jnp.bfloat16),
            jax.ShapeDtypeStruct((1,), jnp.int32),
        ),
        name=f"pack_pairs_{pair_slots}",
    )(row_index[None], cent_index[None], rows, places[None])


def store_part(out_ref, tags, pieces):
    tag_lines = tags.T[:16].astype(jnp.bfloat16)
    slots = tag_lines.shape[1]
    filled = tag_lines[0:1].astype(jnp.float32) > 0.5
    marks = jnp.broadcast_to(filled.astype(jnp.float32), (16, slots)).astype(jnp.bfloat16)
    before = (iota((slots, slots), 0) < iota((slots, slots), 1)).astype(jnp.bfloat16)
    rank = jnp.where(filled, dot(marks, before, 1, 0)[0:1].astype(jnp.int32), -1)
    picks = (iota((PART, slots), 0) == rank).astype(jnp.bfloat16)
    lines = jnp.concatenate([jnp.zeros((8, PART), jnp.float32), dot(tag_lines[:8], picks, 1, 1)], 0)
    first = 0
    for piece in pieces:
        lanes = slice(first, first + piece.shape[1])
        out_ref[:, lanes] = dot(picks, piece, 1, 0).astype(jnp.bfloat16)
        first = first + piece.shape[1]
    kept = out_ref[PART - 16 :, :PART].astype(jnp.float32)
    out_ref[PART - 16 :, :PART] = (kept + lines).astype(jnp.bfloat16)


def compact_pairs_kernel(got_ref, out_ref, *, pair_slots):
    slots = got_ref.shape[0]
    wide = PAIR_TILES[pair_slots]
    tiles = out_ref.shape[1] // LANES
    line = iota((slots, LANES), 0) % PAIR_ROWS
    lane = iota((slots, LANES), 1)
    values = [
        got_ref[:, tile * LANES : (tile + 1) * LANES].astype(jnp.float32) for tile in range(wide)
    ]
    tag_row, lanes = spilled(pair_slots, wide, pair_slots, tiles)
    tags = values[lanes]
    placed = jnp.zeros((slots, LANES), jnp.float32)
    rest = [jnp.zeros((slots, LANES), jnp.float32)] * (tiles - wide)
    for slot in range(pair_slots):
        for tile in range(wide, tiles):
            row, lanes = spilled(slot, tile, pair_slots, tiles)
            moved = pltpu.roll(values[lanes], slots - (row - slot), 0)
            rest[tile - wide] = jnp.where(line == slot, moved, rest[tile - wide])
        moved = pltpu.roll(tags, slots - (tag_row - slot), 0)
        moved = pltpu.roll(moved, (LANES - 2 * slot) % LANES, 1) if slot else moved
        placed = jnp.where((line == slot) & (lane < 2), moved, placed)
    rest = jnp.concatenate(rest, axis=1).astype(jnp.bfloat16)
    store_part(out_ref, placed, [got_ref[...], rest])


def pack_kernel(cent_ref, rows_ref, places_ref, out_ref, *, owner_rows):
    normed = normalise(rows_ref[...])
    count, features = normed.shape
    slots = out_ref.shape[0]
    places = places_ref[0]
    owners = places // owner_rows
    earlier = (as_column(owners) == owners) & (iota((count, count), 0) < iota((count, count), 1))
    rank = jnp.sum(earlier.astype(jnp.int32), axis=0, keepdims=True)
    chosen = (iota((slots, count), 0) == owners * SLOTS + rank).astype(jnp.bfloat16)
    high, low = tag_rows(as_column(places % owner_rows))
    lane = iota((count, LANES), 1)
    tags = jnp.where(lane == 0, high, jnp.where(lane == 1, low, 0))
    tags = tags.astype(jnp.float32).astype(jnp.bfloat16)
    out_ref[:, :features] = dot(chosen, normed, 1, 0).astype(jnp.bfloat16)
    out_ref[:, features:] = dot(chosen, tags, 1, 0).astype(jnp.bfloat16)


def pack(rows, places, cent_index, owners, owner_rows, quarters):
    count, features = rows.shape
    quarter = count // quarters
    slots = owners * SLOTS
    return pl.pallas_call(
        lambda *refs: pack_kernel(*refs, owner_rows=owner_rows),
        grid_spec=pltpu.PrefetchScalarGridSpec(
            num_scalar_prefetch=1,
            grid=(1,),
            in_specs=[
                pl.BlockSpec((quarter, features), lambda i, cent: (cent[0], 0)),
                pl.BlockSpec((1, 1, quarter), lambda i, cent: (cent[0], 0, 0)),
            ],
            out_specs=pl.BlockSpec((slots, features + LANES), lambda i, cent: (0, 0)),
        ),
        out_shape=jax.ShapeDtypeStruct((slots, features + LANES), jnp.bfloat16),
        name="pack",
    )(cent_index[None], rows, places.reshape(quarters, 1, quarter))


def compact_kernel(got_ref, out_ref):
    features = out_ref.shape[1]
    tags = got_ref[:, features:].astype(jnp.float32)
    store_part(out_ref, tags, [got_ref[:, :features]])


def on_chip(array):
    return pltpu.with_memory_space_constraint(array, pltpu.VMEM)


def compacted(kernel, got, features, name):
    return pl.pallas_call(
        kernel,
        in_specs=[pl.BlockSpec(memory_space=pltpu.VMEM)],
        out_shape=pltpu.VMEM((PART, features), jnp.bfloat16),
        name=name,
    )(on_chip(got))


def decoded(high, low):
    places = jnp.where(high > 0.5, (high - 1.0) * float(TAG_BASE) + low, float(NOWHERE))
    return places.astype(jnp.int32)


def part_tags(part_ref):
    return part_ref[PART - 16 :, : 3 * LANES].astype(jnp.float32)


def place_row(part_ref):
    tags = part_tags(part_ref)
    return decoded(tags[8:9, :PART], tags[9:10, :PART])


def place_column(part_ref):
    tags = part_tags(part_ref).T
    return decoded(tags[:PART, 8:9], tags[:PART, 9:10])


def start_row(places, start_lines):
    owner_rows = start_lines.shape[1]
    here = (iota((owner_rows, PART), 0) == places).astype(jnp.bfloat16)
    found = dot(start_lines, here, 1, 0)
    return (found[0:1] * 64.0 + found[1:2]).astype(jnp.int32) - owner_rows


def compared(best, queries_ref, places, starts, key_refs):
    for key_ref, key_places in key_refs:
        similarity = dot(key_ref[...], queries_ref[...], 1, 1)
        allowed = (key_places >= starts) & (key_places < places)
        masked = jnp.where(allowed, similarity, -1.0)
        best = jnp.maximum(best, jnp.max(masked, axis=0, keepdims=True))
    return best


def at_places(best, places, values):
    lines = jnp.concatenate([values, places.astype(jnp.float32)], axis=0)
    lines = jnp.concatenate([lines, jnp.zeros((6, PART), jnp.float32)], axis=0)
    spare = jnp.zeros((8, 3 * LANES - PART), jnp.float32)
    columns = jnp.concatenate([lines, spare], axis=1).T
    owner_rows = best.shape[1]
    there = columns[:PART, 1:2].astype(jnp.int32) == iota((PART, owner_rows), 1)
    placed = jnp.where(there, columns[:PART, 0:1], -1.0)
    return jnp.maximum(best, jnp.max(placed, axis=0, keepdims=True))


def lines_of_starts(starts_ref):
    owner_rows = starts_ref.shape[1]
    starts = starts_ref[...] + owner_rows
    line = iota((16, owner_rows), 0)
    lines = jnp.where(line == 0, starts // 64, jnp.where(line == 1, starts % 64, 0))
    return lines.astype(jnp.float32).astype(jnp.bfloat16)


def store_lines(lines_ref, first, best, places, starts):
    lines_ref[first : first + 1, :] = best
    lines_ref[first + 1 : first + 2, :] = places.astype(jnp.float32)
    lines_ref[first + 2 : first + 3, :] = starts.astype(jnp.float32)


def early_kernel(starts_ref, here_ref, left_ref, previous_ref, lines_ref):
    owner_rows = starts_ref.shape[1]
    start_lines = lines_of_starts(starts_ref)
    here = (here_ref, place_column(here_ref))
    left = (left_ref, place_column(left_ref))
    previous = (previous_ref, place_column(previous_ref) - owner_rows)
    least = jnp.full((1, PART), -1.0, jnp.float32)
    for first, queries_ref, keys in (
        (0, here_ref, (here, left, previous)),
        (3, left_ref, (previous,)),
    ):
        places = place_row(queries_ref)
        starts = start_row(places, start_lines)
        best = compared(least, queries_ref, places, starts, keys)
        store_lines(lines_ref, first, best, places, starts)


def near_kernel(
    starts_ref, early_ref, here_ref, left_ref, right_ref, previous_ref, best_ref, right_lines_ref
):
    owner_rows = starts_ref.shape[1]
    right = (right_ref, place_column(right_ref))
    placed = jnp.full((1, owner_rows), -1.0, jnp.float32)
    for first, queries_ref in ((0, here_ref), (3, left_ref)):
        places = early_ref[first + 1 : first + 2, :].astype(jnp.int32)
        starts = early_ref[first + 2 : first + 3, :].astype(jnp.int32)
        best = early_ref[first : first + 1, :]
        best = compared(best, queries_ref, places, starts, (right,))
        placed = at_places(placed, places, best)
    best_ref[...] = placed
    places = place_row(right_ref)
    starts = start_row(places, lines_of_starts(starts_ref))
    previous = (previous_ref, place_column(previous_ref) - owner_rows)
    least = jnp.full((1, PART), -1.0, jnp.float32)
    best = compared(least, right_ref, places, starts, (previous,))
    store_lines(right_lines_ref, 0, best, places, starts)


def far_kernel(best_ref, right_lines_ref, right_ref, previous_left_ref, out_ref):
    owner_rows = out_ref.shape[1]
    places = right_lines_ref[1:2, :].astype(jnp.int32)
    starts = right_lines_ref[2:3, :].astype(jnp.int32)
    keys = (previous_left_ref, place_column(previous_left_ref) - owner_rows)
    best = compared(right_lines_ref[0:1, :], right_ref, places, starts, (keys,))
    out_ref[...] = at_places(best_ref[...], places, best)


def whole_call(kernel, out_shape, name, *arrays):
    size = sum(array.size for array in arrays)
    return pl.pallas_call(
        kernel,
        in_specs=[pl.BlockSpec(memory_space=pltpu.VMEM)] * len(arrays),
        out_shape=out_shape,
        cost_estimate=pl.CostEstimate(
            flops=2 * size * PART, transcendentals=0, bytes_accessed=8 * size
        ),
        name=name,
    )(*[on_chip(array) for array in arrays])


def margin_of(embeddings, centroids, positions, slab_starts, slab_ends):
    scores = lax.dot_general(
        normalise(embeddings),
        centroids,
        (((1,), (1,)), ((), ())),
        preferred_element_type=jnp.float32,
    )
    best_sim = jnp.max(scores, axis=1)
    assigned = (slab_starts[None, :] <= positions[:, None]) & (
        positions[:, None] < slab_ends[None, :]
    )
    picked = jnp.sum(jnp.where(assigned, scores, 0.0), axis=1)
    both = jnp.stack([best_sim, picked])
    for both_there in [rotated(both, "cent", by) for by in range(1, lax.axis_size("cent"))]:
        best_sim = jnp.maximum(best_sim, both_there[0])
        picked = picked + both_there[1]
    return best_sim - picked


def on_device(embeddings, centroids, positions, cluster_sizes):
    block_rows, features = embeddings.shape
    row_count = lax.axis_size("rows")
    cent_count = lax.axis_size("cent")
    quarter = block_rows // cent_count
    slab_size = centroids.shape[0]
    row_index = lax.axis_index("rows")
    cent_index = lax.axis_index("cent")
    chips = row_count // 2

    def packed_in(pair_slots, embeddings, positions):
        return pack_pairs(
            embeddings, positions, row_index, cent_index, chips, block_rows, pair_slots
        )

    packed, path = packed_in(PAIR_SLOTS[0], embeddings, positions)

    packed, path, cluster_sizes = lax.optimization_barrier((packed, path, cluster_sizes))
    cluster_ends = jnp.cumsum(cluster_sizes)
    cluster_starts = cluster_ends - cluster_sizes
    slab_ends = lax.dynamic_slice_in_dim(cluster_ends, cent_index * slab_size, slab_size)
    slab_starts = lax.dynamic_slice_in_dim(cluster_starts, cent_index * slab_size, slab_size)

    def by_pairs(pair_slots, packed, embeddings, centroids, positions, slab_starts, slab_ends):
        if pair_slots != PAIR_SLOTS[0]:
            packed, _ = packed_in(pair_slots, embeddings, positions)
        got = lax.all_to_all(
            packed,
            "rows",
            split_axis=0,
            concat_axis=0,
            tiled=True,
            axis_index_groups=[list(range(core, row_count, 2)) for core in range(2)],
        )
        margin = margin_of(embeddings, centroids, positions, slab_starts, slab_ends)
        kernel = partial(compact_pairs_kernel, pair_slots=pair_slots)
        return compacted(kernel, got, features, f"compact_pairs_{pair_slots}"), margin

    def by_quarters(packed, embeddings, centroids, positions, slab_starts, slab_ends):
        packed = pack(embeddings, positions, cent_index, row_count, block_rows, cent_count)
        got = lax.all_to_all(
            packed.reshape(row_count, SLOTS, -1), "rows", split_axis=0, concat_axis=0, tiled=True
        )
        margin = margin_of(embeddings, centroids, positions, slab_starts, slab_ends)
        part = compacted(
            compact_kernel, got.reshape(row_count * SLOTS, -1), features, "compact"
        )
        return from_holders(part, 0, 0), margin

    held, margin = lax.switch(
        path[0],
        [partial(by_pairs, pair_slots) for pair_slots in PAIR_SLOTS] + [by_quarters],
        packed,
        embeddings,
        centroids,
        positions,
        slab_starts,
        slab_ends,
    )
    base_place = row_index * block_rows
    places = base_place + jnp.arange(block_rows, dtype=jnp.int32)
    def starts_of(some):
        started = jnp.where(cluster_starts[None, :] <= some[:, None], cluster_starts[None, :], 0)
        return (jnp.max(started, axis=1) - base_place)[None, :]

    first_starts, other_starts = starts_of(places[:LANES]), starts_of(places[LANES:])
    left = from_holders(held, 1, 0)
    held, first_starts = lax.optimization_barrier((held, first_starts))
    right = from_holders(held, 3, 0)
    held, other_starts = lax.optimization_barrier((held, other_starts))
    here = from_holders(held, 0, 0)
    previous_here = from_holders(held, 0, 1)
    starts = jnp.concatenate([first_starts, other_starts], axis=1)
    left, starts = lax.optimization_barrier((left, starts))
    previous_left = to_next_owner(left)
    best_shape = pltpu.VMEM((1, block_rows), jnp.float32)
    early = whole_call(
        early_kernel,
        pltpu.VMEM((6, PART), jnp.float32),
        "early",
        starts,
        here,
        left,
        previous_here,
    )
    best, right_lines = whole_call(
        near_kernel,
        (best_shape, pltpu.VMEM((3, PART), jnp.float32)),
        "near",
        starts,
        early,
        here,
        left,
        right,
        previous_here,
    )
    best = whole_call(
        far_kernel,
        best_shape,
        "far",
        best,
        right_lines,
        right,
        previous_left,
    )
    best = lax.all_to_all(
        best.reshape(cent_count, 2, quarter // 2), "cent", split_axis=0, concat_axis=0, tiled=True
    )
    return (margin, jnp.max(best, axis=0).reshape(quarter))


def solution(mesh):
    in_specs = (P("rows", None), P("cent", None), P("rows"), P())
    out_specs = (P("rows"), P(("rows", "cent")))
    return jax.shard_map(
        on_device, mesh=mesh, in_specs=in_specs, out_specs=out_specs, check_vma=False
    )
```
